256 devices in a mesh: dp: 32 (over x, z_hi, y), ctx: 8 (over z_lo, core).
Axes of the slice: x: 4, y: 4, z: 8 (z_hi: 2, z_lo: 4; z = z_hi * 4 + z_lo), core: 2. Of those that a mesh axis runs over, the one named last changes fastest.
Arguments:
- queries: bfloat16 [32, 2048, 1024], P('dp', 'ctx'), may hold values from -7 to 7
- key_states: bfloat16 [32, 2048, 1024], P('dp', 'ctx'), may hold values from -7 to 7
- value_states: bfloat16 [32, 2048, 1024], P('dp', 'ctx'), may hold values from -6 to 6
- token_order: int32 [32, 2048], P('dp', 'ctx'), may hold values from 0 to 2047, each once within a row
- block_pattern: int32 [32, 16, 4], P('dp'), may hold values from -1 to 15, as said below
- out_weight: bfloat16 [1024, 2048], P('dp'), may hold values from -0.1875 to 0.1875
- out_grad: bfloat16 [32, 2048, 2048], P('dp', 'ctx'), may hold values from -6 to 6
Outputs:
- layer_out: bfloat16 [32, 2048, 2048], P('dp', 'ctx')
- query_grad: bfloat16 [32, 2048, 1024], P('dp', 'ctx')
- key_grad: bfloat16 [32, 2048, 1024], P('dp', 'ctx')
- value_grad: bfloat16 [32, 2048, 1024], P('dp', 'ctx')
- weight_grad: float32 [1024, 2048], P('dp')
The draws below stay inside these ranges and needn't reach their ends.
Inputs may be any that keep to these rules, and one draw needn't show every extreme that they name: `block_pattern`: row b of a session lists key blocks of the same session, each within 2 blocks of b, none twice; slot 0 holds b itself, used slots come before the slots that hold -1, and a row is full whenever 4 blocks lie within that reach.
All inputs are finite; a program needn't handle non-finite values.
Results may differ from the reference program's by a relative error of at most 0.012.
Values may be sent and summed in bfloat16 or wider, within the bound.
A program may use at most 128 MiB of HBM per device.

```python
import math
import jax
import jax.numpy as jnp
from jax import lax

D = 2048
H = 8
HD = 128
BLK = 128
KB = 4
HW = 1024
BATCH = 32
SEQ = 2048
NB = 16
BDEV = 2


def drawn_pair(key):
    draw_shape = (BATCH, SEQ, H, HD)
    query_vals = jnp.clip(jax.random.normal(jax.random.fold_in(key, 1), draw_shape, jnp.float32), -4.0, 4.0)
    key_vals = jnp.clip(jax.random.normal(jax.random.fold_in(key, 2), draw_shape, jnp.float32), -4.0, 4.0)
    return (query_vals.reshape(BATCH, SEQ, H * HD), key_vals.reshape(BATCH, SEQ, H * HD))


def draw_queries(key, part):
    return drawn_pair(key)[0].astype(jnp.bfloat16)


def draw_key_states(key, part):
    return drawn_pair(key)[1].astype(jnp.bfloat16)


def draw_block_pattern(key, part):
    span_width = 2 * BDEV + 1
    offsets = jnp.arange(span_width) - BDEV
    blocks = jnp.arange(NB)[:, None] + offsets[None, :]
    inside = (blocks >= 0) & (blocks < NB)
    noise_ints = jax.random.randint(key, (BATCH, NB, span_width), 0, 1 << 20)
    score_ints = noise_ints * 64 + jnp.arange(span_width)
    score_ints = jnp.where(offsets == 0, 1 << 30, score_ints)
    score_ints = jnp.where(inside, score_ints, -1 - jnp.arange(span_width))
    top_slots = lax.top_k(score_ints, KB)[1]
    chosen = jnp.take_along_axis(jnp.broadcast_to(blocks, (BATCH, NB, span_width)), top_slots, axis=-1)
    usable = jnp.take_along_axis(jnp.broadcast_to(inside, (BATCH, NB, span_width)), top_slots, axis=-1)
    return jnp.where(usable, chosen, -1).astype(jnp.int32)


def block_levels(stream_key, shape, cuts, low, top_value):
    def one(axis_at, parts):
        draws = jax.random.uniform(jax.random.fold_in(jax.random.fold_in(stream_key, 6), axis_at), (parts,), jnp.float32, low / len(cuts), top_value / len(cuts))
        return jnp.repeat(jnp.exp(draws), shape[axis_at] // parts).reshape((-1,) + (1,) * (len(shape) - axis_at - 1))

    level = one(*cuts[0])
    for cut in cuts[1:]:
        level = level * one(*cut)
    return level


def gaussian(stream_key, extent, spread, bound, pieces=(), held_as=jnp.bfloat16):
    level = block_levels(stream_key, extent, pieces, -0.22, 0.18) if pieces else 1.0
    drawn = jax.random.normal(stream_key, extent, jnp.float32) * spread * level
    return jnp.minimum(jnp.maximum(drawn, -bound), bound).astype(held_as)


def setup_inputs(seed: int = 0) -> dict:
    streams_of = jax.random.split(jax.random.key(seed), 8)
    queries = draw_queries(jax.random.fold_in(streams_of[7], 71), 0)
    key_states = draw_key_states(jax.random.fold_in(streams_of[7], 71), 0)
    value_states = gaussian(streams_of[2], (BATCH, SEQ, HW), 1.0, 6.0, ((0, 32), (1, 8)))
    token_order = jax.vmap(lambda own: jax.random.permutation(own, SEQ))(jax.random.split(streams_of[3], BATCH)).reshape((BATCH, SEQ)).astype(jnp.int32)
    block_pattern = draw_block_pattern(jax.random.fold_in(streams_of[7], 71), 0)
    out_weight = gaussian(streams_of[5], (HW, D), HW ** -0.5, 0.1875, ((0, 32),))
    out_grad = gaussian(streams_of[6], (BATCH, SEQ, D), 1.0, 6.0, ((0, 32), (1, 8)))
    return dict(queries=queries, key_states=key_states, value_states=value_states, token_order=token_order, block_pattern=block_pattern, out_weight=out_weight, out_grad=out_grad)


def rope_tables(positions):
    coords = jnp.stack([positions % 8, positions // 8 % 8, positions // 64 % 4, positions // 256], axis=1).astype(jnp.float32)
    per_axis = HD // 16
    frequency = 100.0 ** (-jnp.arange(per_axis, dtype=jnp.float32) / per_axis)
    angle = (coords[:, :, None] * frequency[None, None, :]).reshape(positions.shape[0], 4 * per_axis)
    return (jnp.cos(angle), jnp.sin(angle))

def rotate_heads(heads, cosine, sine_vals, direction):
    quarter = HD // 4
    first_part = heads[..., :quarter]
    second_part = heads[..., quarter:2 * quarter]
    cos_rows = cosine[:, None, :]
    sin_rows = direction * sine_vals[:, None, :]
    return jnp.concatenate([first_part * cos_rows - second_part * sin_rows, second_part * cos_rows + first_part * sin_rows, heads[..., 2 * quarter:]], axis=-1)

def block_sets(table, slots):
    return jnp.take(table, slots, axis=0).reshape(KB * BLK, H, HD)

def session_pass(queries, key_states, value_states, token_order, block_pattern, out_grad, out_weight):
    cosine, sine_vals = rope_tables(token_order)
    rot_query = rotate_heads(queries.astype(jnp.float32).reshape(SEQ, H, HD), cosine, sine_vals, 1.0).astype(jnp.bfloat16)
    rot_keys = rotate_heads(key_states.astype(jnp.float32).reshape(SEQ, H, HD), cosine, sine_vals, 1.0).astype(jnp.bfloat16)
    query_table = rot_query.reshape(NB, BLK, H, HD)
    key_table = rot_keys.reshape(NB, BLK, H, HD)
    value_table = value_states.reshape(NB, BLK, H, HD)
    slot_valid = block_pattern >= 0
    slot_index = jnp.where(slot_valid, block_pattern, 0).astype(jnp.int32)
    score_scale = 1.0 / math.sqrt(HD)

    def block_scores(query_block, slots, valid):
        key_set = block_sets(key_table, slots)
        scores = jnp.einsum('qhd,khd->hqk', query_block.astype(jnp.float32), key_set.astype(jnp.float32)) * score_scale
        key_mask = jnp.repeat(valid, BLK)
        return (jnp.where(key_mask[None, None, :], scores, -jnp.inf), key_set)

    def forward_block(items):
        query_block, slots, valid = items
        scores, key_set = block_scores(query_block, slots, valid)
        value_set = block_sets(value_table, slots)
        row_peak = lax.optimization_barrier(jnp.max(scores, axis=-1))
        row_total = lax.optimization_barrier(jnp.sum(jnp.exp(scores - row_peak[..., None]), axis=-1))
        log_total = row_peak + jnp.log(row_total)
        soft_probs = jnp.exp(scores - log_total[..., None]).astype(jnp.bfloat16)
        block_out = jnp.einsum('hqk,khd->qhd', soft_probs.astype(jnp.float32), value_set.astype(jnp.float32)).astype(jnp.bfloat16)
        return (block_out, log_total)
    block_outs, log_totals = lax.map(forward_block, (query_table, slot_index, slot_valid))
    attn = block_outs.reshape(SEQ, HW)
    layer_out = jnp.dot(attn, out_weight, preferred_element_type=jnp.float32).astype(jnp.bfloat16)
    attn_grad = jnp.dot(out_grad, out_weight.T, preferred_element_type=jnp.float32).astype(jnp.bfloat16)
    weight_term = jnp.dot(attn.T, out_grad, preferred_element_type=jnp.float32)
    grad_dot = lax.optimization_barrier(jnp.sum((attn_grad.astype(jnp.float32) * attn.astype(jnp.float32)).reshape(SEQ, H, HD), axis=-1))
    grad_dot = grad_dot.reshape(NB, BLK, H).transpose(0, 2, 1)
    grad_table = attn_grad.reshape(NB, BLK, H, HD)

    def backward_block(running, items):
        key_sum, value_sum = running
        query_block, slots, valid, log_total, block_dot, grad_block = items
        scores, key_set = block_scores(query_block, slots, valid)
        value_set = block_sets(value_table, slots)
        exact_probs = jnp.exp(scores - log_total[..., None])
        soft_probs = exact_probs.astype(jnp.bfloat16)
        value_part = jnp.einsum('hqk,qhd->khd', soft_probs.astype(jnp.float32), grad_block.astype(jnp.float32))
        prob_grad = jnp.einsum('qhd,khd->hqk', grad_block.astype(jnp.float32), value_set.astype(jnp.float32))
        score_grad = (exact_probs * (prob_grad - block_dot[..., None]) * score_scale).astype(jnp.bfloat16)
        query_part = jnp.einsum('hqk,khd->qhd', score_grad.astype(jnp.float32), key_set.astype(jnp.float32))
        key_part = jnp.einsum('hqk,qhd->khd', score_grad.astype(jnp.float32), query_block.astype(jnp.float32))
        keep = valid.astype(jnp.float32)[:, None, None, None]
        key_sum = key_sum.at[slots].add(key_part.reshape(KB, BLK, H, HD) * keep)
        value_sum = value_sum.at[slots].add(value_part.reshape(KB, BLK, H, HD) * keep)
        return ((key_sum, value_sum), query_part)
    empty = jnp.zeros((NB, BLK, H, HD), jnp.float32)
    (key_sum, value_sum), query_parts = lax.scan(backward_block, (empty, empty), (query_table, slot_index, slot_valid, log_totals, grad_dot, grad_table))
    query_grad = rotate_heads(query_parts.reshape(SEQ, H, HD), cosine, sine_vals, -1.0).reshape(SEQ, HW).astype(jnp.bfloat16)
    key_grad = rotate_heads(key_sum.reshape(SEQ, H, HD), cosine, sine_vals, -1.0).reshape(SEQ, HW).astype(jnp.bfloat16)
    value_grad = value_sum.reshape(SEQ, HW).astype(jnp.bfloat16)
    return (layer_out, query_grad, key_grad, value_grad, weight_term)

def reference(queries, key_states, value_states, token_order, block_pattern, out_weight, out_grad):

    def one_session(running, items):
        outputs = session_pass(items[0], items[1], items[2], items[3], items[4], items[5], out_weight)
        return (running + outputs[4], (outputs[0], outputs[1], outputs[2], outputs[3]))
    start_sum = jnp.zeros((HW, D), jnp.float32)
    weight_sum, stacked = lax.scan(one_session, start_sum, (queries, key_states, value_states, token_order, block_pattern, out_grad))
    return (stacked[0], stacked[1], stacked[2], stacked[3], weight_sum / BATCH)
```

```python
import functools
import math

import jax
import jax.numpy as jnp
from jax import lax
from jax.experimental import pallas as pl
from jax.experimental.pallas import tpu as pltpu
from jax.sharding import PartitionSpec as P

MESH = pl.DeviceIdType.MESH
F32 = jnp.float32
BF16 = jnp.bfloat16
H = 8
HD = 128
BLK = 128
KB = 4
T = 256
NK = 3 * T
D = 2048
HALF = D // 2
ROWS = 32
SCALE = 1.0 / math.sqrt(HD)
NT = (((1,), (1,)), ((), ()))
TN = (((0,), (0,)), ((), ()))
NEG = -1e30


def dot(a, b, dims=(((1,), (0,)), ((), ()))):
    return lax.dot_general(a, b, dims, preferred_element_type=F32)


def rcopy(src, dst, send, recv, device):
    return pltpu.make_async_remote_copy(
        src_ref=src, dst_ref=dst, send_sem=send, recv_sem=recv, device_id=device, device_id_type=MESH
    )


class Gather:
    def __init__(self, unit, pos, f, device, send, recv):
        self.unit = lambda step: unit(lax.rem(pos + step * f + 8, 4))
        self.to = lambda step: device(lax.rem(pos + step * f + 8, 4))
        self.send, self.recv = send, recv

    def copy(self, step, slot, to):
        u = self.unit(step)
        return rcopy(u, u, self.send.at[slot], self.recv.at[slot], self.to(to))

    def start(self):
        self.copy(0, 0, 1).start()
        self.copy(0, 1, -1).start()

    def forward(self):
        self.copy(-1, 0, 1).wait_recv()
        self.copy(-1, 2, 1).start()

    def near(self):
        self.copy(1, 1, -1).wait_recv()

    def far(self):
        self.copy(2, 2, 1).wait_recv()

    def drain(self):
        self.copy(0, 0, 1).wait_send()
        self.copy(0, 1, -1).wait_send()
        self.copy(-1, 2, 1).wait_send()


class Scatter:
    def __init__(self, chunk, pos, f, device, send, recv, bufs):
        self.chunk = lambda step: chunk(lax.rem(pos + step * f + 8, 4))
        self.to = lambda step: device(lax.rem(pos + step * f + 8, 4))
        self.send, self.recv, self.bufs = send, recv, bufs

    def copy(self, src, slot, to):
        return rcopy(src, self.bufs.at[slot], self.send.at[slot], self.recv.at[slot], self.to(to))

    def start(self):
        self.copy(self.chunk(2), 0, 1).start()
        self.copy(self.chunk(-1), 1, -1).start()

    def middle(self):
        self.copy(self.bufs.at[0], 0, 1).wait_recv()
        self.bufs[3] = (self.bufs[0].astype(F32) + self.chunk(1)[...].astype(F32)).astype(BF16)
        self.copy(self.bufs.at[3], 2, 1).start()

    def total(self):
        self.copy(self.bufs.at[1], 1, -1).wait_recv()
        self.copy(self.bufs.at[2], 2, 1).wait_recv()
        return self.chunk(0)[...].astype(F32) + self.bufs[1].astype(F32) + self.bufs[2].astype(F32)

    def drain(self):
        self.copy(self.chunk(2), 0, 1).wait_send()
        self.copy(self.chunk(-1), 1, -1).wait_send()
        self.copy(self.bufs.at[3], 2, 1).wait_send()


def kernel(
    q_hbm, k_hbm, v_hbm, tok_ref, pat_ref, w_hbm, og_hbm,
    lo_hbm, qg_hbm, kg_hbm, vg_hbm, wg_hbm,
    kin, qrot, kv, og, ogs, wb, attn, attns, probs, mask, tabs,
    ret, got, own, qg, kg, vg, lo,
    wg, b1a, b1b, r1a, r1b, b2, zs, zr, fin,
    in_sem, out_sem, halo_s, halo_r, ret_s, ret_r, sib_s, sib_r, wz_s, wz_r,
    ag_s, ag_r, wsib_s, wsib_r, rs_s, rs_r, z_s, z_r, fin_s, fin_r,
):
    dp = lax.axis_index("dp")
    ctx = lax.axis_index("ctx")
    x, zh, y = dp // 8, lax.rem(dp // 4, 2), lax.rem(dp, 4)
    zl, core = ctx // 2, lax.rem(ctx, 2)
    z = zh * 4 + zl
    line = z * 2 + core
    f = 1 - 2 * core

    def device(x_, z_, y_, core_):
        return (x_ * 8 + (z_ // 4) * 4 + y_, lax.rem(z_, 4) * 2 + core_)

    def on_line(at):
        return device(x, at // 2, y, lax.rem(at, 2))

    left, right = on_line(lax.rem(line + 15, 16)), on_line(lax.rem(line + 1, 16))
    sibling = (dp, ctx + f)
    on_x = lambda at: device(at, z, y, core)
    on_y = lambda at: device(x, z, at, core)

    def head_cols(h):
        return pl.ds(h * HD, HD)

    ins = []

    def load(src, dst, sem):
        c = pltpu.make_async_copy(src, dst, in_sem.at[sem])
        c.start()
        return c

    my_half = pl.ds(pl.multiple_of(core * HALF, HALF), HALF)
    in_w = load(w_hbm.at[:, my_half], wb.at[x, zh, y, core], 0)
    in_k = [load(k_hbm.at[:, head_cols(h)], kin.at[h], 1 + h) for h in range(H)]
    in_v = [load(v_hbm.at[:, head_cols(h)], kv.at[h, 1, 1], 9 + h) for h in range(H)]
    in_og = load(og_hbm, og, 17)
    in_q = [load(q_hbm.at[:, head_cols(h)], qrot.at[h], 18 + h) for h in range(H)]

    barrier = pltpu.get_barrier_semaphore()
    for step in range(1, 16):
        pl.semaphore_signal(barrier, inc=1, device_id=on_line(lax.rem(line + step, 16)), device_id_type=MESH)
    for step in (1, 3):
        pl.semaphore_signal(barrier, inc=1, device_id=on_x(lax.rem(x + step, 4)), device_id_type=MESH)
        pl.semaphore_signal(barrier, inc=1, device_id=on_y(lax.rem(y + step, 4)), device_id_type=MESH)

    lane8 = lax.broadcasted_iota(jnp.int32, (8, HD), 1)
    value = lax.broadcasted_iota(jnp.int32, (8, HD), 0).astype(F32)
    freq = jnp.exp(lax.rem(lane8, 8).astype(F32) * (-math.log(100.0) / 8.0))
    cos_of, sin_of = jnp.cos(value * freq), jnp.sin(value * freq)
    tok = jnp.transpose(jnp.broadcast_to(tok_ref[...].astype(F32), (HD, T))).astype(jnp.int32)
    lane = lax.broadcasted_iota(jnp.int32, (T, HD), 1)
    axis = lax.rem(lane, 32) // 8
    shift = jnp.where(axis < 3, axis * 3, 8)
    coord = lax.shift_right_logical(tok, shift) & jnp.where(axis == 2, 3, 7)

    def look_up(table):
        rows = [table[i : i + 1, :] for i in range(8)]
        for bit in range(3):
            on = (coord & (1 << bit)) != 0
            rows = [jnp.where(on, rows[2 * i + 1], rows[2 * i]) for i in range(len(rows) // 2)]
        return rows[0]

    sine = look_up(sin_of)
    tabs[0] = jnp.where(lane < 64, look_up(cos_of), 1.0)
    tabs[1] = jnp.where(lane < 32, -sine, 0.0)
    tabs[2] = jnp.where((lane >= 32) & (lane < 64), sine, 0.0)

    def rotate(v, sign):
        side = pltpu.roll(v, 96, 1) * tabs[1] + pltpu.roll(v, 32, 1) * tabs[2]
        return v * tabs[0] + side if sign > 0 else v * tabs[0] - side

    for i in range(2):
        b = ctx * 2 + i
        for r in range(6):
            kb = ctx * 2 - 2 + r
            hit = (pat_ref[b, 0] == kb) | (pat_ref[b, 1] == kb) | (pat_ref[b, 2] == kb) | (pat_ref[b, 3] == kb)
            fill = jnp.where(hit & (kb >= 0), 0.0, NEG)
            mask[pl.ds(i * BLK, BLK), pl.ds(r * BLK, BLK)] = jnp.full((BLK, BLK), fill, F32)

    in_w.wait()
    pl.semaphore_wait(barrier, 19)

    wz = rcopy(wb.at[x, zh, y, core], wb.at[x, zh, y, core], wz_s, wz_r, device(x, 7 - z, y, core))
    wz.start()
    gathers = []
    for s in range(2):
        half = zh if s == 0 else 1 - zh
        top, bottom = pl.ds(0, 16), pl.ds(16, 16)
        first = (
            Gather(lambda p, half=half, top=top: wb.at[x, half, p, core, top], y, f, on_y, ag_s.at[s, 0], ag_r.at[s, 0]),
            Gather(lambda p, half=half, bottom=bottom: wb.at[p, half, y, core, bottom], x, f, on_x, ag_s.at[s, 1], ag_r.at[s, 1]),
        )
        second = (
            Gather(lambda p, half=half, top=top: wb.at[p, half, :, core, top], x, f, on_x, ag_s.at[s, 2], ag_r.at[s, 2]),
            Gather(lambda p, half=half, bottom=bottom: wb.at[:, half, p, core, bottom], y, f, on_y, ag_s.at[s, 3], ag_r.at[s, 3]),
        )
        gathers.append((first, second))

    def share(s, step, who=None):
        half = zh if s == 0 else 1 - zh
        at = core if who is None else who
        px, py = lax.rem(x + step * f + 8, 4), lax.rem(y + step * f + 8, 4)
        a = wb.at[px, half, :, at, pl.ds(0, 16)]
        c = wb.at[:, half, py, at, pl.ds(16, 16)]
        k = step % 4
        return (
            rcopy(a, a, wsib_s.at[s, 0, k], wsib_r.at[s, 0, k], sibling),
            rcopy(c, c, wsib_s.at[s, 1, k], wsib_r.at[s, 1, k], sibling),
        )

    def send_share(s, step):
        for c in share(s, step):
            c.start()

    for g in gathers[0][0]:
        g.start()

    def halo(h):
        return (
            rcopy(kv.at[h, 1], kv.at[h, 2], halo_s.at[0, h], halo_r.at[0, h], left),
            rcopy(kv.at[h, 1], kv.at[h, 0], halo_s.at[1, h], halo_r.at[1, h], right),
        )

    for h in range(H):
        in_k[h].wait()
        kv[h, 1, 0] = rotate(kin[h].astype(F32), 1).astype(BF16)
        in_v[h].wait()
        if h:
            for c in halo(h - 1):
                c.start()
    in_og.wait()
    for c in halo(H - 1):
        c.start()
    other_half = pl.ds(pl.multiple_of((1 - core) * HALF, HALF), HALF)
    ogc = rcopy(og.at[:, other_half], ogs, sib_s.at[8], sib_r.at[8], sibling)
    ogc.start()

    def attn_copy(h):
        return rcopy(attn.at[h], attns.at[h], sib_s.at[h], sib_r.at[h], sibling)

    for h in range(H):
        in_q[h].wait()
        qrot[h] = rotate(qrot[h].astype(F32), 1).astype(BF16)

    for g in gathers[0][0]:
        g.forward()
    wz.wait_recv()
    for g in gathers[1][0]:
        g.start()

    def second_ring(s):
        for g in gathers[s][0]:
            g.near()
            g.far()
        for g in gathers[s][1]:
            g.start()
        send_share(s, 0)

    second_ring(0)

    def keys(h):
        return kv[h, :, 0].reshape(NK, HD)

    def values(h):
        return kv[h, :, 1].reshape(NK, HD)

    def forward(h, carry):
        for c in halo(h):
            c.wait_recv()
        scores = dot(qrot[h], keys(h), NT) * SCALE + mask[...]
        e = jnp.exp(scores - jnp.max(scores, axis=1, keepdims=True))
        p = (e * (1.0 / jnp.sum(e, axis=1, keepdims=True))).astype(BF16)
        probs[h] = p
        attn[h] = dot(p, values(h)).astype(BF16)

        @pl.when(h == 1)
        def _():
            for g in gathers[1][0]:
                g.forward()

        @pl.when(h == 2)
        def _():
            second_ring(1)

        @pl.when(h == 4)
        def _():
            for g in gathers[0][1]:
                g.forward()
            send_share(0, -1)
            for g in gathers[0][1]:
                g.near()
            send_share(0, 1)

        @pl.when(h == 6)
        def _():
            for g in gathers[1][1]:
                g.forward()
            send_share(1, -1)
            for g in gathers[1][1]:
                g.near()
            send_share(1, 1)

        attn_copy(h).start()
        return carry

    lax.fori_loop(0, H, forward, 0)
    for s in range(2):
        for g in gathers[s][1]:
            g.far()
        send_share(s, 2)

    ogc.wait_recv()

    def weight_term(h, carry):
        attn_copy(h).wait_recv()
        term = dot(attn[h], og[:, my_half], TN) + dot(attns[h], ogs[...], TN)
        wg[h // 2, lax.rem(h, 2)] = (term * (1.0 / 32.0)).astype(BF16).reshape(4, ROWS, HALF)
        return carry

    lax.fori_loop(0, H, weight_term, 0)

    scatters = []
    for s in range(2):
        scatters.append((
            Scatter(lambda p, s=s: wg.at[p, s, :, pl.ds(0, 16)], x, f, on_x, rs_s.at[s, 0], rs_r.at[s, 0], b1a.at[s]),
            Scatter(lambda p, s=s: wg.at[:, s, p, pl.ds(16, 16)], y, f, on_y, rs_s.at[s, 1], rs_r.at[s, 1], b1b.at[s]),
            Scatter(lambda p, s=s: r1a.at[s, p], y, f, on_y, rs_s.at[s, 2], rs_r.at[s, 2], b2.at[s, 0]),
            Scatter(lambda p, s=s: r1b.at[s, p], x, f, on_x, rs_s.at[s, 3], rs_r.at[s, 3], b2.at[s, 1]),
        ))
    for s in range(2):
        scatters[s][0].start()
        scatters[s][1].start()

    for s in range(2):
        for k in range(4):
            step = k if k < 3 else -1
            for c in share(s, step, 1 - core):
                c.wait_recv()

    def give_back(h):
        return (
            rcopy(ret.at[0, h], got.at[1, h], ret_s.at[0, h], ret_r.at[1, h], left),
            rcopy(ret.at[1, h], got.at[0, h], ret_s.at[1, h], ret_r.at[0, h], right),
        )

    def take_back(h):
        return (
            rcopy(ret.at[0, h], got.at[1, h], ret_s.at[0, h], ret_r.at[1, h], right),
            rcopy(ret.at[1, h], got.at[0, h], ret_s.at[1, h], ret_r.at[0, h], left),
        )

    def backward(h, carry):
        w = wb.at[h // 2, lax.rem(h, 2)]
        grad = (
            dot(og[:, :HALF], w[:, 0].reshape(HD, HALF), NT) + dot(og[:, HALF:], w[:, 1].reshape(HD, HALF), NT)
        ).astype(BF16)
        delta = jnp.sum(grad.astype(F32) * attn[h].astype(F32), axis=1, keepdims=True)
        p = probs[h]
        dv = dot(p, grad, TN)
        ret[0, h, 1] = dv[:T].astype(BF16)
        own[h, 1] = dv[T : 2 * T]
        ret[1, h, 1] = dv[2 * T :].astype(BF16)
        ds = (p.astype(F32) * ((dot(grad, values(h), NT) - delta) * SCALE)).astype(BF16)
        dk = dot(ds, qrot[h], TN)
        ret[0, h, 0] = dk[:T].astype(BF16)
        own[h, 0] = dk[T : 2 * T]
        ret[1, h, 0] = dk[2 * T :].astype(BF16)
        qg[h] = rotate(dot(ds, keys(h)), -1).astype(BF16)
        for c in give_back(h):
            c.start()

        @pl.when(h == 3)
        def _():
            for s in range(2):
                scatters[s][0].middle()
                scatters[s][1].middle()

        return carry

    lax.fori_loop(0, H, backward, 0)

    outs = []

    def store(src, dst, sem):
        c = pltpu.make_async_copy(src, dst, out_sem.at[sem])
        c.start()
        outs.append(c)

    for h in range(H):
        store(qg.at[h], qg_hbm.at[:, head_cols(h)], h)

    def reduce_plane():
        for s in range(2):
            r1a[s] = scatters[s][0].total().astype(BF16)
            scatters[s][2].start()
            r1b[s] = scatters[s][1].total().astype(BF16)
            scatters[s][3].start()

    reduce_plane()
    for s in range(2):
        scatters[s][2].middle()
        scatters[s][3].middle()

    rows = jnp.concatenate([attn[h] for h in range(H)], axis=1)

    def project(j, carry):
        cols = pl.ds(pl.multiple_of(lax.rem(j, 4) * 256, 256), 256)
        w = wb[:, :, :, j // 4, :, cols].reshape(H * HD, 256)
        lo[:, pl.ds(pl.multiple_of(j * 256, 256), 256)] = dot(rows, w).astype(BF16)
        return carry

    lax.fori_loop(0, 8, project, 0)
    store(lo, lo_hbm, 8)

    for s in range(2):
        for part in range(2):
            done = scatters[s][2 + part].total().astype(BF16)
            for j in range(4):
                zs[s * 4 + j, pl.ds(part * 16, 16)] = done[:, j * 256 : (j + 1) * 256]

    def z_copy(step):
        to = lax.rem(z + step, 8)
        return rcopy(zs.at[to], zr.at[step - 1], z_s.at[step - 1], z_r.at[step - 1], device(x, to, y, core))

    for step in range(1, 8):
        z_copy(step).start()

    def finish(h, carry):
        for c in take_back(h):
            c.wait_recv()
        dk = own[h, 0] + got[0, h, 0].astype(F32) + got[1, h, 0].astype(F32)
        dv = own[h, 1] + got[0, h, 1].astype(F32) + got[1, h, 1].astype(F32)
        kg[h] = rotate(dk, -1).astype(BF16)
        vg[h] = dv.astype(BF16)
        return carry

    lax.fori_loop(0, H, finish, 0)
    for h in range(H):
        store(kg.at[h], kg_hbm.at[:, head_cols(h)], 9 + h)
        store(vg.at[h], vg_hbm.at[:, head_cols(h)], 17 + h)

    for step in range(1, 8):
        z_copy(step).wait_recv()
    total = zs[z].astype(F32)
    for step in range(7):
        total = total + zr[step].astype(F32)
    fin[ctx] = total

    def fin_copy(step):
        to = lax.rem(ctx + step, 8)
        return rcopy(fin.at[ctx], fin.at[ctx], fin_s.at[step - 1], fin_r.at[step - 1], (dp, to))

    def fin_from(step):
        who = lax.rem(ctx + 8 - step, 8)
        return rcopy(fin.at[who], fin.at[who], fin_s.at[step - 1], fin_r.at[step - 1], (dp, who))

    for step in range(1, 8):
        fin_copy(step).start()
    for step in range(1, 8):
        fin_from(step).wait_recv()
    for c in range(8):
        store(fin.at[c], wg_hbm.at[:, pl.ds((c % 2) * HALF + (c // 2) * 256, 256)], 25 + c)

    wz.wait_send()
    ogc.wait_send()
    for h in range(H):
        attn_copy(h).wait_send()
        for c in (*halo(h), *give_back(h)):
            c.wait_send()
    for s in range(2):
        for g in (*gathers[s][0], *gathers[s][1], *scatters[s]):
            g.drain()
        for k in range(4):
            for c in share(s, k if k < 3 else -1):
                c.wait_send()
    for step in range(1, 8):
        z_copy(step).wait_send()
        fin_copy(step).wait_send()
    for c in outs:
        c.wait()


def shards(queries, key_states, value_states, token_order, block_pattern, out_weight, out_grad):
    any_ = pl.BlockSpec(memory_space=pl.ANY)
    vmem = pl.BlockSpec(memory_space=pltpu.VMEM)
    smem = pl.BlockSpec(memory_space=pltpu.SMEM)
    dma = pltpu.SemaphoreType.DMA
    V = pltpu.VMEM
    token_rows = jax.ShapeDtypeStruct((T, H * HD), BF16)
    out = pl.pallas_call(
        kernel,
        out_shape=(
            jax.ShapeDtypeStruct((T, D), BF16),
            token_rows,
            token_rows,
            token_rows,
            jax.ShapeDtypeStruct((ROWS, D), F32),
        ),
        in_specs=[any_, any_, any_, vmem, smem, any_, any_],
        out_specs=(any_,) * 5,
        scratch_shapes=[
            V((H, T, HD), BF16),
            V((H, T, HD), BF16),
            V((H, 3, 2, T, HD), BF16),
            V((T, D), BF16),
            V((T, HALF), BF16),
            V((4, 2, 4, 2, ROWS, HALF), BF16),
            V((H, T, HD), BF16),
            V((H, T, HD), BF16),
            V((H, T, NK), BF16),
            V((T, NK), F32),
            V((3, T, HD), F32),
            V((2, H, 2, T, HD), BF16),
            V((2, H, 2, T, HD), BF16),
            V((H, 2, T, HD), F32),
            V((H, T, HD), BF16),
            V((H, T, HD), BF16),
            V((H, T, HD), BF16),
            V((T, D), BF16),
            V((4, 2, 4, ROWS, HALF), BF16),
            V((2, 4, 4, 16, HALF), BF16),
            V((2, 4, 4, 16, HALF), BF16),
            V((2, 4, 16, HALF), BF16),
            V((2, 4, 16, HALF), BF16),
            V((2, 2, 4, 16, HALF), BF16),
            V((8, ROWS, 256), BF16),
            V((7, ROWS, 256), BF16),
            V((8, ROWS, 256), F32),
            dma((26,)), dma((33,)),
            dma((2, H)), dma((2, H)), dma((2, H)), dma((2, H)),
            dma((9,)), dma((9,)), dma(()), dma(()),
            dma((2, 4, 3)), dma((2, 4, 3)), dma((2, 2, 4)), dma((2, 2, 4)),
            dma((2, 4, 3)), dma((2, 4, 3)), dma((7,)), dma((7,)), dma((7,)), dma((7,)),
        ],
        compiler_params=pltpu.CompilerParams(
            collective_id=0, has_side_effects=True, vmem_limit_bytes=60 * 1024 * 1024
        ),
    )(
        queries[0], key_states[0], value_states[0], token_order, block_pattern[0], out_weight, out_grad[0]
    )
    lo, qg, kg, vg, wg = out
    return lo[None], qg[None], kg[None], vg[None], wg


def solution(mesh):
    rows = P("dp", "ctx", None)
    in_specs = (rows, rows, rows, P("dp", "ctx"), P("dp", None, None), P("dp", None), rows)
    out_specs = (rows, rows, rows, rows, P("dp", None))
    return jax.shard_map(shards, mesh=mesh, in_specs=in_specs, out_specs=out_specs, check_vma=False)
```

```python
import functools
import math

import jax
import jax.numpy as jnp
from jax import lax
from jax.experimental import pallas as pl
from jax.experimental.pallas import tpu as pltpu
from jax.sharding import PartitionSpec as P

MESH = pl.DeviceIdType.MESH
F32 = jnp.float32
BF16 = jnp.bfloat16
H = 8
HD = 128
BLK = 128
KB = 4
T = 256
NK = 3 * T
D = 2048
HALF = D // 2
ROWS = 32
SCALE = 1.0 / math.sqrt(HD)
NT = (((1,), (1,)), ((), ()))
TN = (((0,), (0,)), ((), ()))
NEG = -1e30
LIMIT = 40 * 1024 * 1024


def dot(a, b, dims=(((1,), (0,)), ((), ()))):
    return lax.dot_general(a, b, dims, preferred_element_type=F32)


def rcopy(src, dst, send, recv, device):
    return pltpu.make_async_remote_copy(
        src_ref=src, dst_ref=dst, send_sem=send, recv_sem=recv, device_id=device, device_id_type=MESH
    )


class Gather:
    def __init__(self, unit, pos, f, device, send, recv):
        self.unit = lambda step: unit(lax.rem(pos + step * f + 8, 4))
        self.to = lambda step: device(lax.rem(pos + step * f + 8, 4))
        self.send, self.recv = send, recv

    def copy(self, step, slot, to):
        u = self.unit(step)
        return rcopy(u, u, self.send.at[slot], self.recv.at[slot], self.to(to))

    def start(self):
        self.copy(0, 0, 1).start()
        self.copy(0, 1, -1).start()

    def forward(self):
        self.copy(-1, 0, 1).wait_recv()
        self.copy(-1, 2, 1).start()

    def near(self):
        self.copy(1, 1, -1).wait_recv()

    def far(self):
        self.copy(2, 2, 1).wait_recv()

    def drain(self):
        self.copy(0, 0, 1).wait_send()
        self.copy(0, 1, -1).wait_send()
        self.copy(-1, 2, 1).wait_send()


class Scatter:
    def __init__(self, chunk, pos, f, device, send, recv, bufs):
        self.chunk = lambda step: chunk(lax.rem(pos + step * f + 8, 4))
        self.to = lambda step: device(lax.rem(pos + step * f + 8, 4))
        self.send, self.recv, self.bufs = send, recv, bufs

    def copy(self, src, slot, to):
        return rcopy(src, self.bufs.at[slot], self.send.at[slot], self.recv.at[slot], self.to(to))

    def start(self):
        self.copy(self.chunk(2), 0, 1).start()
        self.copy(self.chunk(-1), 1, -1).start()

    def middle(self):
        self.copy(self.bufs.at[0], 0, 1).wait_recv()
        self.bufs[3] = (self.bufs[0].astype(F32) + self.chunk(1)[...].astype(F32)).astype(BF16)
        self.copy(self.bufs.at[3], 2, 1).start()

    def total(self):
        self.copy(self.bufs.at[1], 1, -1).wait_recv()
        self.copy(self.bufs.at[2], 2, 1).wait_recv()
        return self.chunk(0)[...].astype(F32) + self.bufs[1].astype(F32) + self.bufs[2].astype(F32)

    def drain(self):
        self.copy(self.chunk(2), 0, 1).wait_send()
        self.copy(self.chunk(-1), 1, -1).wait_send()
        self.copy(self.bufs.at[3], 2, 1).wait_send()


def kernel(
    q_hbm, k_hbm, v_hbm, tok_ref, pat_ref, w_hbm, og_hbm,
    lo, qg, kg, vg, fin,
    kin, qrot, kv, og, ogs, wb, attn, attns, probs, mask, tabs,
    ret, got, own,
    wg, b1a, b1b, r1a, r1b, b2, zs, zr,
    in_sem, halo_s, halo_r, ret_s, ret_r, sib_s, sib_r, wz_s, wz_r,
    ag_s, ag_r, wsib_s, wsib_r, rs_s, rs_r, z_s, z_r, fin_s, fin_r,
):
    dp = lax.axis_index("dp")
    ctx = lax.axis_index("ctx")
    x, zh, y = dp // 8, lax.rem(dp // 4, 2), lax.rem(dp, 4)
    zl, core = ctx // 2, lax.rem(ctx, 2)
    z = zh * 4 + zl
    line = z * 2 + core
    f = 1 - 2 * core

    def device(x_, z_, y_, core_):
        return (x_ * 8 + (z_ // 4) * 4 + y_, lax.rem(z_, 4) * 2 + core_)

    def on_line(at):
        return device(x, at // 2, y, lax.rem(at, 2))

    left, right = on_line(lax.rem(line + 15, 16)), on_line(lax.rem(line + 1, 16))
    sibling = (dp, ctx + f)
    on_x = lambda at: device(at, z, y, core)
    on_y = lambda at: device(x, z, at, core)

    def head_cols(h):
        return pl.ds(h * HD, HD)

    ins = []

    def load(src, dst, sem):
        c = pltpu.make_async_copy(src, dst, in_sem.at[sem])
        c.start()
        return c

    my_half = pl.ds(pl.multiple_of(core * HALF, HALF), HALF)
    in_w = load(w_hbm.at[:, my_half], wb.at[x, zh, y, core], 0)
    in_k = [load(k_hbm.at[:, head_cols(h)], kin.at[h], 1 + h) for h in range(H)]
    in_v = [load(v_hbm.at[:, head_cols(h)], kv.at[h, 1, 1], 9 + h) for h in range(H)]
    in_og = load(og_hbm, og, 17)
    in_q = [load(q_hbm.at[:, head_cols(h)], qrot.at[h], 18 + h) for h in range(H)]

    barrier = pltpu.get_barrier_semaphore()
    for step in range(1, 16):
        pl.semaphore_signal(barrier, inc=1, device_id=on_line(lax.rem(line + step, 16)), device_id_type=MESH)
    for step in (1, 3):
        pl.semaphore_signal(barrier, inc=1, device_id=on_x(lax.rem(x + step, 4)), device_id_type=MESH)
        pl.semaphore_signal(barrier, inc=1, device_id=on_y(lax.rem(y + step, 4)), device_id_type=MESH)

    lane8 = lax.broadcasted_iota(jnp.int32, (8, HD), 1)
    value = lax.broadcasted_iota(jnp.int32, (8, HD), 0).astype(F32)
    freq = jnp.exp(lax.rem(lane8, 8).astype(F32) * (-math.log(100.0) / 8.0))
    cos_of, sin_of = jnp.cos(value * freq), jnp.sin(value * freq)
    tok = jnp.transpose(jnp.broadcast_to(tok_ref[...].astype(F32), (HD, T))).astype(jnp.int32)
    lane = lax.broadcasted_iota(jnp.int32, (T, HD), 1)
    axis = lax.rem(lane, 32) // 8
    shift = jnp.where(axis < 3, axis * 3, 8)
    coord = lax.shift_right_logical(tok, shift) & jnp.where(axis == 2, 3, 7)

    def look_up(table):
        rows = [table[i : i + 1, :] for i in range(8)]
        for bit in range(3):
            on = (coord & (1 << bit)) != 0
            rows = [jnp.where(on, rows[2 * i + 1], rows[2 * i]) for i in range(len(rows) // 2)]
        return rows[0]

    sine = look_up(sin_of)
    tabs[0] = jnp.where(lane < 64, look_up(cos_of), 1.0)
    tabs[1] = jnp.where(lane < 32, -sine, 0.0)
    tabs[2] = jnp.where((lane >= 32) & (lane < 64), sine, 0.0)

    def rotate(v, sign):
        side = pltpu.roll(v, 96, 1) * tabs[1] + pltpu.roll(v, 32, 1) * tabs[2]
        return v * tabs[0] + side if sign > 0 else v * tabs[0] - side

    for i in range(2):
        b = ctx * 2 + i
        for r in range(6):
            kb = ctx * 2 - 2 + r
            hit = (pat_ref[0, b] == kb) | (pat_ref[1, b] == kb) | (pat_ref[2, b] == kb) | (pat_ref[3, b] == kb)
            fill = jnp.where(hit & (kb >= 0), 0.0, NEG)
            mask[pl.ds(i * BLK, BLK), pl.ds(r * BLK, BLK)] = jnp.full((BLK, BLK), fill, F32)

    in_w.wait()
    pl.semaphore_wait(barrier, 19)

    wz = rcopy(wb.at[x, zh, y, core], wb.at[x, zh, y, core], wz_s, wz_r, device(x, 7 - z, y, core))
    wz.start()
    gathers = []
    for s in range(2):
        half = zh if s == 0 else 1 - zh
        top, bottom = pl.ds(0, 16), pl.ds(16, 16)
        first = (
            Gather(lambda p, half=half, top=top: wb.at[x, half, p, core, top], y, f, on_y, ag_s.at[s, 0], ag_r.at[s, 0]),
            Gather(lambda p, half=half, bottom=bottom: wb.at[p, half, y, core, bottom], x, f, on_x, ag_s.at[s, 1], ag_r.at[s, 1]),
        )
        second = (
            Gather(lambda p, half=half, top=top: wb.at[p, half, :, core, top], x, f, on_x, ag_s.at[s, 2], ag_r.at[s, 2]),
            Gather(lambda p, half=half, bottom=bottom: wb.at[:, half, p, core, bottom], y, f, on_y, ag_s.at[s, 3], ag_r.at[s, 3]),
        )
        gathers.append((first, second))

    def share(s, step, who=None):
        half = zh if s == 0 else 1 - zh
        at = core if who is None else who
        px, py = lax.rem(x + step * f + 8, 4), lax.rem(y + step * f + 8, 4)
        a = wb.at[px, half, :, at, pl.ds(0, 16)]
        c = wb.at[:, half, py, at, pl.ds(16, 16)]
        k = step % 4
        return (
            rcopy(a, a, wsib_s.at[s, 0, k], wsib_r.at[s, 0, k], sibling),
            rcopy(c, c, wsib_s.at[s, 1, k], wsib_r.at[s, 1, k], sibling),
        )

    def send_share(s, step):
        for c in share(s, step):
            c.start()

    for g in gathers[0][0]:
        g.start()

    def halo(h):
        return (
            rcopy(kv.at[h, 1], kv.at[h, 2], halo_s.at[0, h], halo_r.at[0, h], left),
            rcopy(kv.at[h, 1], kv.at[h, 0], halo_s.at[1, h], halo_r.at[1, h], right),
        )

    for h in range(H):
        in_k[h].wait()
        kv[h, 1, 0] = rotate(kin[h].astype(F32), 1).astype(BF16)
        in_v[h].wait()
        if h:
            for c in halo(h - 1):
                c.start()
    in_og.wait()
    for c in halo(H - 1):
        c.start()
    other_half = pl.ds(pl.multiple_of((1 - core) * HALF, HALF), HALF)
    ogc = rcopy(og.at[:, other_half], ogs, sib_s.at[8], sib_r.at[8], sibling)
    ogc.start()

    def attn_copy(h):
        return rcopy(attn.at[h], attns.at[h], sib_s.at[h], sib_r.at[h], sibling)

    for h in range(H):
        in_q[h].wait()
        qrot[h] = rotate(qrot[h].astype(F32), 1).astype(BF16)

    for g in gathers[0][0]:
        g.forward()
    wz.wait_recv()
    for g in gathers[1][0]:
        g.start()

    def second_ring(s):
        for g in gathers[s][0]:
            g.near()
            g.far()
        for g in gathers[s][1]:
            g.start()
        send_share(s, 0)

    second_ring(0)

    def keys(h):
        return kv[h, :, 0].reshape(NK, HD)

    def values(h):
        return kv[h, :, 1].reshape(NK, HD)

    def forward(i, carry):
        heads = [2 * i, 2 * i + 1]
        for h in heads:
            for c in halo(h):
                c.wait_recv()
        done = []
        for h in heads:
            scores = dot(qrot[h], keys(h), NT) * SCALE + mask[...]
            e = jnp.exp(scores - jnp.max(scores, axis=1, keepdims=True))
            p = (e * (1.0 / jnp.sum(e, axis=1, keepdims=True))).astype(BF16)
            done.append((p, dot(p, values(h)).astype(BF16)))
        for h, (p, a) in zip(heads, done):
            probs[h] = p
            attn[h] = a

        @pl.when(i == 0)
        def _():
            for g in gathers[1][0]:
                g.forward()

        @pl.when(i == 1)
        def _():
            second_ring(1)

        @pl.when(i == 2)
        def _():
            for g in gathers[0][1]:
                g.forward()
            send_share(0, -1)
            for g in gathers[0][1]:
                g.near()
            send_share(0, 1)

        @pl.when(i == 3)
        def _():
            for g in gathers[1][1]:
                g.forward()
            send_share(1, -1)
            for g in gathers[1][1]:
                g.near()
            send_share(1, 1)

        for h in heads:
            attn_copy(h).start()
        return carry

    lax.fori_loop(0, H // 2, forward, 0)
    for s in range(2):
        for g in gathers[s][1]:
            g.far()
        send_share(s, 2)

    ogc.wait_recv()

    def weight_term(h, carry):
        attn_copy(h).wait_recv()
        term = dot(attn[h], og[:, my_half], TN) + dot(attns[h], ogs[...], TN)
        wg[h // 2, lax.rem(h, 2)] = (term * (1.0 / 32.0)).astype(BF16).reshape(4, ROWS, HALF)
        return carry

    lax.fori_loop(0, H, weight_term, 0)

    scatters = []
    for s in range(2):
        scatters.append((
            Scatter(lambda p, s=s: wg.at[p, s, :, pl.ds(0, 16)], x, f, on_x, rs_s.at[s, 0], rs_r.at[s, 0], b1a.at[s]),
            Scatter(lambda p, s=s: wg.at[:, s, p, pl.ds(16, 16)], y, f, on_y, rs_s.at[s, 1], rs_r.at[s, 1], b1b.at[s]),
            Scatter(lambda p, s=s: r1a.at[s, p], y, f, on_y, rs_s.at[s, 2], rs_r.at[s, 2], b2.at[s, 0]),
            Scatter(lambda p, s=s: r1b.at[s, p], x, f, on_x, rs_s.at[s, 3], rs_r.at[s, 3], b2.at[s, 1]),
        ))
    for s in range(2):
        scatters[s][0].start()
        scatters[s][1].start()

    for s in range(2):
        for k in range(4):
            step = k if k < 3 else -1
            for c in share(s, step, 1 - core):
                c.wait_recv()

    def give_back(h):
        return (
            rcopy(ret.at[0, h], got.at[1, h], ret_s.at[0, h], ret_r.at[1, h], left),
            rcopy(ret.at[1, h], got.at[0, h], ret_s.at[1, h], ret_r.at[0, h], right),
        )

    def take_back(h):
        return (
            rcopy(ret.at[0, h], got.at[1, h], ret_s.at[0, h], ret_r.at[1, h], right),
            rcopy(ret.at[1, h], got.at[0, h], ret_s.at[1, h], ret_r.at[0, h], left),
        )

    def reduce_plane(s):
        r1a[s] = scatters[s][0].total().astype(BF16)
        scatters[s][2].start()
        r1b[s] = scatters[s][1].total().astype(BF16)
        scatters[s][3].start()

    def middle(s, ring):
        for part in range(2):
            scatters[s][2 * ring + part].middle()

    def backward(i, carry):
        w = wb.at[i]
        heads = [2 * i, 2 * i + 1]
        grads = (
            dot(og[:, :HALF], w[:, :, 0].reshape(2 * HD, HALF), NT)
            + dot(og[:, HALF:], w[:, :, 1].reshape(2 * HD, HALF), NT)
        ).astype(BF16)
        done = []
        for n, h in enumerate(heads):
            grad = grads[:, n * HD : (n + 1) * HD]
            delta = jnp.sum(grad.astype(F32) * attn[h].astype(F32), axis=1, keepdims=True)
            p = probs[h]
            dv = dot(p, grad, TN)
            ds = (p.astype(F32) * ((dot(grad, values(h), NT) - delta) * SCALE)).astype(BF16)
            dk = dot(ds, qrot[h], TN)
            done.append((dv, dk, rotate(dot(ds, keys(h)), -1).astype(BF16)))
        for h, (dv, dk, dq) in zip(heads, done):
            ret[0, h, 1] = dv[:T].astype(BF16)
            own[h, 1] = dv[T : 2 * T]
            ret[1, h, 1] = dv[2 * T :].astype(BF16)
            ret[0, h, 0] = dk[:T].astype(BF16)
            own[h, 0] = dk[T : 2 * T]
            ret[1, h, 0] = dk[2 * T :].astype(BF16)
            qg[h] = dq
        for h in heads:
            for c in give_back(h):
                c.start()

        @pl.when(i == 2)
        def _():
            middle(0, 0)
            middle(1, 0)

        return carry

    lax.fori_loop(0, H // 2, backward, 0)
    reduce_plane(0)
    reduce_plane(1)

    rows = jnp.concatenate([attn[h] for h in range(H)], axis=1)

    def project(j, carry):
        cols = pl.ds(pl.multiple_of(lax.rem(j, 4) * 256, 256), 256)
        w = wb[:, :, :, j // 4, :, cols].reshape(H * HD, 256)
        lo[:, pl.ds(pl.multiple_of(j * 256, 256), 256)] = dot(rows, w).astype(BF16)

        @pl.when(j == 3)
        def _():
            middle(0, 1)
            middle(1, 1)

        return carry

    lax.fori_loop(0, 8, project, 0)

    for s in range(2):
        for part in range(2):
            done = scatters[s][2 + part].total().astype(BF16)
            for j in range(4):
                zs[s * 4 + j, pl.ds(part * 16, 16)] = done[:, j * 256 : (j + 1) * 256]

    def z_copy(step):
        to = lax.rem(z + step, 8)
        return rcopy(zs.at[to], zr.at[step - 1], z_s.at[step - 1], z_r.at[step - 1], device(x, to, y, core))

    for step in range(1, 8):
        z_copy(step).start()

    def finish(h, carry):
        for c in take_back(h):
            c.wait_recv()
        dk = own[h, 0] + got[0, h, 0].astype(F32) + got[1, h, 0].astype(F32)
        dv = own[h, 1] + got[0, h, 1].astype(F32) + got[1, h, 1].astype(F32)
        kg[h] = rotate(dk, -1).astype(BF16)
        vg[h] = dv.astype(BF16)
        return carry

    lax.fori_loop(0, H, finish, 0)
    for step in range(1, 8):
        z_copy(step).wait_recv()
    total = zs[z].astype(F32)
    for step in range(7):
        total = total + zr[step].astype(F32)
    fin[ctx] = total

    def fin_copy(step):
        to = lax.rem(ctx + step, 8)
        return rcopy(fin.at[ctx], fin.at[ctx], fin_s.at[step - 1], fin_r.at[step - 1], (dp, to))

    def fin_from(step):
        who = lax.rem(ctx + 8 - step, 8)
        return rcopy(fin.at[who], fin.at[who], fin_s.at[step - 1], fin_r.at[step - 1], (dp, who))

    for step in range(1, 8):
        fin_copy(step).start()
    for step in range(1, 8):
        fin_from(step).wait_recv()

    wz.wait_send()
    ogc.wait_send()
    for h in range(H):
        attn_copy(h).wait_send()
        for c in (*halo(h), *give_back(h)):
            c.wait_send()
    for s in range(2):
        for g in (*gathers[s][0], *gathers[s][1], *scatters[s]):
            g.drain()
        for k in range(4):
            for c in share(s, k if k < 3 else -1):
                c.wait_send()
    for step in range(1, 8):
        z_copy(step).wait_send()
        fin_copy(step).wait_send()


def write(lo, qg, kg, vg, fin, lo_hbm, qg_hbm, kg_hbm, vg_hbm, wg_hbm, sem):
    copies = [(lo, lo_hbm)]
    for h in range(H):
        cols = pl.ds(h * HD, HD)
        for src, dst in ((qg, qg_hbm), (kg, kg_hbm), (vg, vg_hbm)):
            copies.append((src.at[h], dst.at[:, cols]))
    for c in range(8):
        copies.append((fin.at[c], wg_hbm.at[:, pl.ds((c % 2) * HALF + (c // 2) * 256, 256)]))
    copies = [pltpu.make_async_copy(src, dst, sem.at[i]) for i, (src, dst) in enumerate(copies)]
    for c in copies:
        c.start()
    for c in copies:
        c.wait()


def shards(queries, key_states, value_states, token_order, block_pattern, out_weight, out_grad):
    any_ = pl.BlockSpec(memory_space=pl.ANY)
    hbm = lambda array: pltpu.with_memory_space_constraint(array, pltpu.HBM)
    vmem = pl.BlockSpec(memory_space=pltpu.VMEM)
    smem = pl.BlockSpec(memory_space=pltpu.SMEM)
    dma = pltpu.SemaphoreType.DMA
    V = pltpu.VMEM
    token_rows = jax.ShapeDtypeStruct((T, H * HD), BF16)
    out = pl.pallas_call(
        kernel,
        out_shape=(
            V((T, D), BF16),
            V((H, T, HD), BF16),
            V((H, T, HD), BF16),
            V((H, T, HD), BF16),
            V((8, ROWS, 256), F32),
        ),
        in_specs=[any_, any_, any_, vmem, smem, any_, any_],
        out_specs=(vmem,) * 5,
        scratch_shapes=[
            V((H, T, HD), BF16),
            V((H, T, HD), BF16),
            V((H, 3, 2, T, HD), BF16),
            V((T, D), BF16),
            V((T, HALF), BF16),
            V((4, 2, 4, 2, ROWS, HALF), BF16),
            V((H, T, HD), BF16),
            V((H, T, HD), BF16),
            V((H, T, NK), BF16),
            V((T, NK), F32),
            V((3, T, HD), F32),
            V((2, H, 2, T, HD), BF16),
            V((2, H, 2, T, HD), BF16),
            V((H, 2, T, HD), F32),
            V((4, 2, 4, ROWS, HALF), BF16),
            V((2, 4, 4, 16, HALF), BF16),
            V((2, 4, 4, 16, HALF), BF16),
            V((2, 4, 16, HALF), BF16),
            V((2, 4, 16, HALF), BF16),
            V((2, 2, 4, 16, HALF), BF16),
            V((8, ROWS, 256), BF16),
            V((7, ROWS, 256), BF16),
            dma((26,)),
            dma((2, H)), dma((2, H)), dma((2, H)), dma((2, H)),
            dma((9,)), dma((9,)), dma(()), dma(()),
            dma((2, 4, 3)), dma((2, 4, 3)), dma((2, 2, 4)), dma((2, 2, 4)),
            dma((2, 4, 3)), dma((2, 4, 3)), dma((7,)), dma((7,)), dma((7,)), dma((7,)),
        ],
        compiler_params=pltpu.CompilerParams(
            collective_id=0, has_side_effects=True, vmem_limit_bytes=LIMIT
        ),
    )(
        hbm(queries[0]),
        hbm(key_states[0]),
        hbm(value_states[0]),
        token_order,
        jnp.transpose(block_pattern[0]),
        hbm(out_weight),
        hbm(out_grad[0]),
    )
    lo, qg, kg, vg, wg = pl.pallas_call(
        write,
        out_shape=(
            jax.ShapeDtypeStruct((T, D), BF16),
            token_rows,
            token_rows,
            token_rows,
            jax.ShapeDtypeStruct((ROWS, D), F32),
        ),
        in_specs=[vmem] * 5,
        out_specs=(any_,) * 5,
        scratch_shapes=[dma((33,))],
        compiler_params=pltpu.CompilerParams(vmem_limit_bytes=LIMIT),
    )(*(pltpu.with_memory_space_constraint(o, pltpu.VMEM) for o in out))
    return lo[None], qg[None], kg[None], vg[None], wg


def solution(mesh):
    rows = P("dp", "ctx", None)
    in_specs = (rows, rows, rows, P("dp", "ctx"), P("dp", None, None), P("dp", None), rows)
    out_specs = (rows, rows, rows, rows, P("dp", None))
    return jax.shard_map(shards, mesh=mesh, in_specs=in_specs, out_specs=out_specs, check_vma=False)
```

```python
import functools
import math

import jax
import jax.numpy as jnp
from jax import lax
from jax.experimental import pallas as pl
from jax.experimental.pallas import tpu as pltpu
from jax.sharding import PartitionSpec as P

MESH = pl.DeviceIdType.MESH
F32 = jnp.float32
BF16 = jnp.bfloat16
H = 8
HD = 128
BLK = 128
KB = 4
T = 256
NK = 3 * T
D = 2048
HALF = D // 2
ROWS = 32
SCALE = 1.0 / math.sqrt(HD)
NT = (((1,), (1,)), ((), ()))
TN = (((0,), (0,)), ((), ()))
NEG = -1e30
LIMIT = 40 * 1024 * 1024


def dot(a, b, dims=(((1,), (0,)), ((), ()))):
    return lax.dot_general(a, b, dims, preferred_element_type=F32)


def rcopy(src, dst, send, recv, device):
    return pltpu.make_async_remote_copy(
        src_ref=src, dst_ref=dst, send_sem=send, recv_sem=recv, device_id=device, device_id_type=MESH
    )


class Gather:
    def __init__(self, unit, pos, f, device, send, recv, direct=False):
        self.direct = direct
        self.unit = lambda step: unit(lax.rem(pos + step * f + 8, 4))
        self.to = lambda step: device(lax.rem(pos + step * f + 8, 4))
        self.send, self.recv = send, recv

    def copy(self, step, slot, to):
        u = self.unit(step)
        return rcopy(u, u, self.send.at[slot], self.recv.at[slot], self.to(to))

    def start(self):
        self.copy(0, 0, 1).start()
        self.copy(0, 1, -1).start()
        if self.direct:
            self.copy(0, 2, 2).start()

    def forward(self):
        self.copy(-1, 0, 1).wait_recv()
        if not self.direct:
            self.copy(-1, 2, 1).start()

    def near(self):
        self.copy(1, 1, -1).wait_recv()

    def far(self):
        self.copy(2, 2, 1).wait_recv()

    def drain(self):
        self.copy(0, 0, 1).wait_send()
        self.copy(0, 1, -1).wait_send()
        if self.direct:
            self.copy(0, 2, 2).wait_send()
        else:
            self.copy(-1, 2, 1).wait_send()


class Scatter:
    def __init__(self, chunk, pos, f, device, send, recv, bufs):
        self.chunk = lambda step: chunk(lax.rem(pos + step * f + 8, 4))
        self.to = lambda step: device(lax.rem(pos + step * f + 8, 4))
        self.send, self.recv, self.bufs = send, recv, bufs

    def copy(self, src, slot, to):
        return rcopy(src, self.bufs.at[slot], self.send.at[slot], self.recv.at[slot], self.to(to))

    def start(self):
        self.copy(self.chunk(2), 0, 1).start()
        self.copy(self.chunk(-1), 1, -1).start()

    def middle(self):
        self.copy(self.bufs.at[0], 0, 1).wait_recv()
        self.bufs[3] = (self.bufs[0].astype(F32) + self.chunk(1)[...].astype(F32)).astype(BF16)
        self.copy(self.bufs.at[3], 2, 1).start()

    def total(self):
        self.copy(self.bufs.at[1], 1, -1).wait_recv()
        self.copy(self.bufs.at[2], 2, 1).wait_recv()
        return self.chunk(0)[...].astype(F32) + self.bufs[1].astype(F32) + self.bufs[2].astype(F32)

    def drain(self):
        self.copy(self.chunk(2), 0, 1).wait_send()
        self.copy(self.chunk(-1), 1, -1).wait_send()
        self.copy(self.bufs.at[3], 2, 1).wait_send()


def kernel(
    q_hbm, k_hbm, v_hbm, tok_ref, pat_ref, w_hbm, og_hbm,
    lo, qg, kg, vg, fin,
    kin, qrot, kv, og, ogs, wb, attn, attns, probs, mask, tabs,
    ret, got, own,
    wg, b1a, b1b, r1a, r1b, b2, zs, zr,
    in_sem, halo_s, halo_r, ret_s, ret_r, sib_s, sib_r, wz_s, wz_r,
    ag_s, ag_r, wsib_s, wsib_r, rs_s, rs_r, z_s, z_r, fin_s, fin_r,
):
    dp = lax.axis_index("dp")
    ctx = lax.axis_index("ctx")
    x, zh, y = dp // 8, lax.rem(dp // 4, 2), lax.rem(dp, 4)
    zl, core = ctx // 2, lax.rem(ctx, 2)
    z = zh * 4 + zl
    line = z * 2 + core
    f = 1 - 2 * core

    def device(x_, z_, y_, core_):
        return (x_ * 8 + (z_ // 4) * 4 + y_, lax.rem(z_, 4) * 2 + core_)

    def on_line(at):
        return device(x, at // 2, y, lax.rem(at, 2))

    left, right = on_line(lax.rem(line + 15, 16)), on_line(lax.rem(line + 1, 16))
    sibling = (dp, ctx + f)
    on_x = lambda at: device(at, z, y, core)
    on_y = lambda at: device(x, z, at, core)

    def head_cols(h):
        return pl.ds(h * HD, HD)

    ins = []

    def load(src, dst, sem):
        c = pltpu.make_async_copy(src, dst, in_sem.at[sem])
        c.start()
        return c

    my_half = pl.ds(pl.multiple_of(core * HALF, HALF), HALF)
    in_w = load(w_hbm.at[:, my_half], wb.at[x, zh, y, core], 0)
    in_k = [load(k_hbm.at[:, head_cols(h)], kin.at[h], 1 + h) for h in range(H)]
    in_v = [load(v_hbm.at[:, head_cols(h)], kv.at[h, 1, 1], 9 + h) for h in range(H)]
    in_og = load(og_hbm, og, 17)
    in_q = [load(q_hbm.at[:, head_cols(h)], qrot.at[h], 18 + h) for h in range(H)]

    barrier = pltpu.get_barrier_semaphore()
    for step in range(1, 16):
        pl.semaphore_signal(barrier, inc=1, device_id=on_line(lax.rem(line + step, 16)), device_id_type=MESH)
    for step in range(1, 4):
        pl.semaphore_signal(barrier, inc=1, device_id=on_x(lax.rem(x + step, 4)), device_id_type=MESH)
        pl.semaphore_signal(barrier, inc=1, device_id=on_y(lax.rem(y + step, 4)), device_id_type=MESH)

    lane8 = lax.broadcasted_iota(jnp.int32, (8, HD), 1)
    value = lax.broadcasted_iota(jnp.int32, (8, HD), 0).astype(F32)
    freq = jnp.exp(lax.rem(lane8, 8).astype(F32) * (-math.log(100.0) / 8.0))
    cos_of, sin_of = jnp.cos(value * freq), jnp.sin(value * freq)
    tok = jnp.transpose(jnp.broadcast_to(tok_ref[...].astype(F32), (HD, T))).astype(jnp.int32)
    lane = lax.broadcasted_iota(jnp.int32, (T, HD), 1)
    axis = lax.rem(lane, 32) // 8
    shift = jnp.where(axis < 3, axis * 3, 8)
    coord = lax.shift_right_logical(tok, shift) & jnp.where(axis == 2, 3, 7)

    def look_up(table):
        rows = [table[i : i + 1, :] for i in range(8)]
        for bit in range(3):
            on = (coord & (1 << bit)) != 0
            rows = [jnp.where(on, rows[2 * i + 1], rows[2 * i]) for i in range(len(rows) // 2)]
        return rows[0]

    sine = look_up(sin_of)
    tabs[0] = jnp.where(lane < 64, look_up(cos_of), 1.0)
    tabs[1] = jnp.where(lane < 32, -sine, 0.0)
    tabs[2] = jnp.where((lane >= 32) & (lane < 64), sine, 0.0)

    def rotate(v, sign):
        side = pltpu.roll(v, 96, 1) * tabs[1] + pltpu.roll(v, 32, 1) * tabs[2]
        return v * tabs[0] + side if sign > 0 else v * tabs[0] - side

    for i in range(2):
        b = ctx * 2 + i
        for r in range(6):
            kb = ctx * 2 - 2 + r
            hit = (pat_ref[0, b] == kb) | (pat_ref[1, b] == kb) | (pat_ref[2, b] == kb) | (pat_ref[3, b] == kb)
            fill = jnp.where(hit & (kb >= 0), 0.0, NEG)
            mask[pl.ds(i * BLK, BLK), pl.ds(r * BLK, BLK)] = jnp.full((BLK, BLK), fill, F32)

    in_w.wait()
    pl.semaphore_wait(barrier, 21)

    wz = rcopy(wb.at[x, zh, y, core], wb.at[x, zh, y, core], wz_s, wz_r, device(x, 7 - z, y, core))
    wz.start()
    gathers = []
    for s in range(2):
        half = zh if s == 0 else 1 - zh
        top, bottom = pl.ds(0, 16), pl.ds(16, 16)
        first = (
            Gather(lambda p, half=half, top=top: wb.at[x, half, p, core, top], y, f, on_y, ag_s.at[s, 0], ag_r.at[s, 0], True),
            Gather(lambda p, half=half, bottom=bottom: wb.at[p, half, y, core, bottom], x, f, on_x, ag_s.at[s, 1], ag_r.at[s, 1], True),
        )
        second = (
            Gather(lambda p, half=half, top=top: wb.at[p, half, :, core, top], x, f, on_x, ag_s.at[s, 2], ag_r.at[s, 2]),
            Gather(lambda p, half=half, bottom=bottom: wb.at[:, half, p, core, bottom], y, f, on_y, ag_s.at[s, 3], ag_r.at[s, 3]),
        )
        gathers.append((first, second))

    def share(s, step, who=None):
        half = zh if s == 0 else 1 - zh
        at = core if who is None else who
        px, py = lax.rem(x + step * f + 8, 4), lax.rem(y + step * f + 8, 4)
        a = wb.at[px, half, :, at, pl.ds(0, 16)]
        c = wb.at[:, half, py, at, pl.ds(16, 16)]
        k = step % 4
        return (
            rcopy(a, a, wsib_s.at[s, 0, k], wsib_r.at[s, 0, k], sibling),
            rcopy(c, c, wsib_s.at[s, 1, k], wsib_r.at[s, 1, k], sibling),
        )

    def send_share(s, step):
        for c in share(s, step):
            c.start()

    for g in gathers[0][0]:
        g.start()

    def halo(h):
        return (
            rcopy(kv.at[h, 1], kv.at[h, 2], halo_s.at[0, h], halo_r.at[0, h], left),
            rcopy(kv.at[h, 1], kv.at[h, 0], halo_s.at[1, h], halo_r.at[1, h], right),
        )

    for h in range(H):
        in_k[h].wait()
        kv[h, 1, 0] = rotate(kin[h].astype(F32), 1).astype(BF16)
        in_v[h].wait()
        if h:
            for c in halo(h - 1):
                c.start()
    in_og.wait()
    for c in halo(H - 1):
        c.start()
    other_half = pl.ds(pl.multiple_of((1 - core) * HALF, HALF), HALF)
    ogc = rcopy(og.at[:, other_half], ogs, sib_s.at[8], sib_r.at[8], sibling)
    ogc.start()

    def attn_copy(h):
        return rcopy(attn.at[h], attns.at[h], sib_s.at[h], sib_r.at[h], sibling)

    for h in range(H):
        in_q[h].wait()
        qrot[h] = rotate(qrot[h].astype(F32), 1).astype(BF16)

    wz.wait_recv()
    for g in gathers[1][0]:
        g.start()

    def second_ring(s):
        for g in gathers[s][0]:
            g.forward()
            g.near()
            g.far()
        for g in gathers[s][1]:
            g.start()
        send_share(s, 0)

    second_ring(0)

    def keys(h):
        return kv[h, :, 0].reshape(NK, HD)

    def values(h):
        return kv[h, :, 1].reshape(NK, HD)

    def forward(i, carry):
        heads = [2 * i, 2 * i + 1]
        for h in heads:
            for c in halo(h):
                c.wait_recv()
        done = []
        for h in heads:
            scores = dot(qrot[h], keys(h), NT) * SCALE + mask[...]
            e = jnp.exp(scores - jnp.max(scores, axis=1, keepdims=True))
            p = (e * (1.0 / jnp.sum(e, axis=1, keepdims=True))).astype(BF16)
            done.append((p, dot(p, values(h)).astype(BF16)))
        for h, (p, a) in zip(heads, done):
            probs[h] = p
            attn[h] = a

        def relay(s):
            for g in gathers[s][1]:
                g.forward()
            send_share(s, -1)

        def near(s):
            for g in gathers[s][1]:
                g.near()
            send_share(s, 1)

        @pl.when(i == 0)
        def _():
            second_ring(1)

        @pl.when(i == 1)
        def _():
            relay(0)

        @pl.when(i == 2)
        def _():
            near(0)
            relay(1)

        @pl.when(i == 3)
        def _():
            near(1)

        for h in heads:
            attn_copy(h).start()
        return carry

    lax.fori_loop(0, H // 2, forward, 0)
    for s in range(2):
        for g in gathers[s][1]:
            g.far()
        send_share(s, 2)

    ogc.wait_recv()

    def weight_term(h, carry):
        attn_copy(h).wait_recv()
        term = dot(attn[h], og[:, my_half], TN) + dot(attns[h], ogs[...], TN)
        wg[h // 2, lax.rem(h, 2)] = (term * (1.0 / 32.0)).astype(BF16).reshape(4, ROWS, HALF)
        return carry

    lax.fori_loop(0, H, weight_term, 0)

    scatters = []
    for s in range(2):
        scatters.append((
            Scatter(lambda p, s=s: wg.at[p, s, :, pl.ds(0, 16)], x, f, on_x, rs_s.at[s, 0], rs_r.at[s, 0], b1a.at[s]),
            Scatter(lambda p, s=s: wg.at[:, s, p, pl.ds(16, 16)], y, f, on_y, rs_s.at[s, 1], rs_r.at[s, 1], b1b.at[s]),
            Scatter(lambda p, s=s: r1a.at[s, p], y, f, on_y, rs_s.at[s, 2], rs_r.at[s, 2], b2.at[s, 0]),
            Scatter(lambda p, s=s: r1b.at[s, p], x, f, on_x, rs_s.at[s, 3], rs_r.at[s, 3], b2.at[s, 1]),
        ))
    for s in range(2):
        scatters[s][0].start()
        scatters[s][1].start()

    for s in range(2):
        for k in range(4):
            step = k if k < 3 else -1
            for c in share(s, step, 1 - core):
                c.wait_recv()

    def give_back(h):
        return (
            rcopy(ret.at[0, h], got.at[1, h], ret_s.at[0, h], ret_r.at[1, h], left),
            rcopy(ret.at[1, h], got.at[0, h], ret_s.at[1, h], ret_r.at[0, h], right),
        )

    def take_back(h):
        return (
            rcopy(ret.at[0, h], got.at[1, h], ret_s.at[0, h], ret_r.at[1, h], right),
            rcopy(ret.at[1, h], got.at[0, h], ret_s.at[1, h], ret_r.at[0, h], left),
        )

    def reduce_plane(s):
        r1a[s] = scatters[s][0].total().astype(BF16)
        scatters[s][2].start()
        r1b[s] = scatters[s][1].total().astype(BF16)
        scatters[s][3].start()

    def middle(s, ring):
        for part in range(2):
            scatters[s][2 * ring + part].middle()

    def backward(i, carry):
        w = wb.at[i]
        heads = [2 * i, 2 * i + 1]
        grads = (
            dot(og[:, :HALF], w[:, :, 0].reshape(2 * HD, HALF), NT)
            + dot(og[:, HALF:], w[:, :, 1].reshape(2 * HD, HALF), NT)
        ).astype(BF16)
        done = []
        for n, h in enumerate(heads):
            grad = grads[:, n * HD : (n + 1) * HD]
            delta = jnp.sum(grad.astype(F32) * attn[h].astype(F32), axis=1, keepdims=True)
            p = probs[h]
            dv = dot(p, grad, TN)
            ds = (p.astype(F32) * ((dot(grad, values(h), NT) - delta) * SCALE)).astype(BF16)
            dk = dot(ds, qrot[h], TN)
            done.append((dv, dk, rotate(dot(ds, keys(h)), -1).astype(BF16)))
        for h, (dv, dk, dq) in zip(heads, done):
            ret[0, h, 1] = dv[:T].astype(BF16)
            own[h, 1] = dv[T : 2 * T]
            ret[1, h, 1] = dv[2 * T :].astype(BF16)
            ret[0, h, 0] = dk[:T].astype(BF16)
            own[h, 0] = dk[T : 2 * T]
            ret[1, h, 0] = dk[2 * T :].astype(BF16)
            qg[h] = dq
        for h in heads:
            for c in give_back(h):
                c.start()

        @pl.when(i == 1)
        def _():
            middle(0, 0)

        @pl.when(i == 2)
        def _():
            middle(1, 0)

        return carry

    lax.fori_loop(0, H // 2, backward, 0)
    reduce_plane(0)
    reduce_plane(1)

    rows = jnp.concatenate([attn[h] for h in range(H)], axis=1)

    def project(j, carry):
        cols = pl.ds(pl.multiple_of(lax.rem(j, 4) * 256, 256), 256)
        w = wb[:, :, :, j // 4, :, cols].reshape(H * HD, 256)
        lo[:, pl.ds(pl.multiple_of(j * 256, 256), 256)] = dot(rows, w).astype(BF16)

        return carry

    lax.fori_loop(0, 3, project, 0)
    for s in range(2):
        middle(s, 1)

    def finish(h, carry):
        for c in take_back(h):
            c.wait_recv()
        dk = own[h, 0] + got[0, h, 0].astype(F32) + got[1, h, 0].astype(F32)
        dv = own[h, 1] + got[0, h, 1].astype(F32) + got[1, h, 1].astype(F32)
        kg[h] = rotate(dk, -1).astype(BF16)
        vg[h] = dv.astype(BF16)
        return carry

    lax.fori_loop(0, H, finish, 0)

    for s in range(2):
        for part in range(2):
            done = scatters[s][2 + part].total().astype(BF16)
            for j in range(4):
                zs[s * 4 + j, pl.ds(part * 16, 16)] = done[:, j * 256 : (j + 1) * 256]

    def z_copy(step):
        to = lax.rem(z + step, 8)
        return rcopy(zs.at[to], zr.at[step - 1], z_s.at[step - 1], z_r.at[step - 1], device(x, to, y, core))

    for step in range(1, 8):
        z_copy(step).start()

    lax.fori_loop(3, 8, project, 0)
    for step in range(1, 8):
        z_copy(step).wait_recv()
    total = zs[z].astype(F32)
    for step in range(7):
        total = total + zr[step].astype(F32)
    fin[ctx] = total.astype(BF16)

    def fin_copy(step):
        to = lax.rem(ctx + step, 8)
        return rcopy(fin.at[ctx], fin.at[ctx], fin_s.at[step - 1], fin_r.at[step - 1], (dp, to))

    def fin_from(step):
        who = lax.rem(ctx + 8 - step, 8)
        return rcopy(fin.at[who], fin.at[who], fin_s.at[step - 1], fin_r.at[step - 1], (dp, who))

    for step in range(1, 8):
        fin_copy(step).start()
    for step in range(1, 8):
        fin_from(step).wait_recv()

    wz.wait_send()
    ogc.wait_send()
    for h in range(H):
        attn_copy(h).wait_send()
        for c in (*halo(h), *give_back(h)):
            c.wait_send()
    for s in range(2):
        for g in (*gathers[s][0], *gathers[s][1], *scatters[s]):
            g.drain()
        for k in range(4):
            for c in share(s, k if k < 3 else -1):
                c.wait_send()
    for step in range(1, 8):
        z_copy(step).wait_send()
        fin_copy(step).wait_send()


def write(lo, qg, kg, vg, fin, lo_hbm, qg_hbm, kg_hbm, vg_hbm, wg_hbm, wide, sem):
    copies = []

    def store(src, dst):
        copies.append(pltpu.make_async_copy(src, dst, sem.at[len(copies)]))
        copies[-1].start()

    store(lo, lo_hbm)
    for h in range(H):
        cols = pl.ds(h * HD, HD)
        for src, dst in ((qg, qg_hbm), (kg, kg_hbm), (vg, vg_hbm)):
            store(src.at[h], dst.at[:, cols])
    wide[...] = fin[...].astype(F32)
    for c in range(8):
        store(wide.at[c], wg_hbm.at[:, pl.ds((c % 2) * HALF + (c // 2) * 256, 256)])
    for c in copies:
        c.wait()


def shards(queries, key_states, value_states, token_order, block_pattern, out_weight, out_grad):
    any_ = pl.BlockSpec(memory_space=pl.ANY)
    hbm = lambda array: pltpu.with_memory_space_constraint(array, pltpu.HBM)
    vmem = pl.BlockSpec(memory_space=pltpu.VMEM)
    smem = pl.BlockSpec(memory_space=pltpu.SMEM)
    dma = pltpu.SemaphoreType.DMA
    V = pltpu.VMEM
    token_rows = jax.ShapeDtypeStruct((T, H * HD), BF16)
    out = pl.pallas_call(
        kernel,
        out_shape=(
            V((T, D), BF16),
            V((H, T, HD), BF16),
            V((H, T, HD), BF16),
            V((H, T, HD), BF16),
            V((8, ROWS, 256), BF16),
        ),
        in_specs=[any_, any_, any_, vmem, smem, any_, any_],
        out_specs=(vmem,) * 5,
        scratch_shapes=[
            V((H, T, HD), BF16),
            V((H, T, HD), BF16),
            V((H, 3, 2, T, HD), BF16),
            V((T, D), BF16),
            V((T, HALF), BF16),
            V((4, 2, 4, 2, ROWS, HALF), BF16),
            V((H, T, HD), BF16),
            V((H, T, HD), BF16),
            V((H, T, NK), BF16),
            V((T, NK), F32),
            V((3, T, HD), F32),
            V((2, H, 2, T, HD), BF16),
            V((2, H, 2, T, HD), BF16),
            V((H, 2, T, HD), F32),
            V((4, 2, 4, ROWS, HALF), BF16),
            V((2, 4, 4, 16, HALF), BF16),
            V((2, 4, 4, 16, HALF), BF16),
            V((2, 4, 16, HALF), BF16),
            V((2, 4, 16, HALF), BF16),
            V((2, 2, 4, 16, HALF), BF16),
            V((8, ROWS, 256), BF16),
            V((7, ROWS, 256), BF16),
            dma((26,)),
            dma((2, H)), dma((2, H)), dma((2, H)), dma((2, H)),
            dma((9,)), dma((9,)), dma(()), dma(()),
            dma((2, 4, 3)), dma((2, 4, 3)), dma((2, 2, 4)), dma((2, 2, 4)),
            dma((2, 4, 3)), dma((2, 4, 3)), dma((7,)), dma((7,)), dma((7,)), dma((7,)),
        ],
        compiler_params=pltpu.CompilerParams(
            collective_id=0, has_side_effects=True, vmem_limit_bytes=LIMIT
        ),
    )(
        hbm(queries[0]),
        hbm(key_states[0]),
        hbm(value_states[0]),
        token_order,
        jnp.transpose(block_pattern[0]),
        hbm(out_weight),
        hbm(out_grad[0]),
    )
    lo, qg, kg, vg, wg = pl.pallas_call(
        write,
        out_shape=(
            jax.ShapeDtypeStruct((T, D), BF16),
            token_rows,
            token_rows,
            token_rows,
            jax.ShapeDtypeStruct((ROWS, D), F32),
        ),
        in_specs=[vmem] * 5,
        out_specs=(any_,) * 5,
        scratch_shapes=[V((8, ROWS, 256), F32), dma((33,))],
        compiler_params=pltpu.CompilerParams(vmem_limit_bytes=LIMIT),
    )(*(pltpu.with_memory_space_constraint(o, pltpu.VMEM) for o in out))
    return lo[None], qg[None], kg[None], vg[None], wg


def solution(mesh):
    rows = P("dp", "ctx", None)
    in_specs = (rows, rows, rows, P("dp", "ctx"), P("dp", None, None), P("dp", None), rows)
    out_specs = (rows, rows, rows, rows, P("dp", None))
    return jax.shard_map(shards, mesh=mesh, in_specs=in_specs, out_specs=out_specs, check_vma=False)
```

```python
import functools
import math

import jax
import jax.numpy as jnp
from jax import lax
from jax.experimental import pallas as pl
from jax.experimental.pallas import tpu as pltpu
from jax.sharding import PartitionSpec as P

MESH = pl.DeviceIdType.MESH
F32 = jnp.float32
BF16 = jnp.bfloat16
H = 8
HD = 128
BLK = 128
KB = 4
T = 256
NK = 3 * T
D = 2048
HALF = D // 2
ROWS = 32
SCALE = 1.0 / math.sqrt(HD)
NT = (((1,), (1,)), ((), ()))
TN = (((0,), (0,)), ((), ()))
NEG = -1e30
LIMIT = 40 * 1024 * 1024


def dot(a, b, dims=(((1,), (0,)), ((), ()))):
    return lax.dot_general(a, b, dims, preferred_element_type=F32)


def rcopy(src, dst, send, recv, device):
    return pltpu.make_async_remote_copy(
        src_ref=src, dst_ref=dst, send_sem=send, recv_sem=recv, device_id=device, device_id_type=MESH
    )


class Gather:
    def __init__(self, unit, pos, f, device, send, recv, direct=False):
        self.direct = direct
        self.unit = lambda step: unit(lax.rem(pos + step * f + 8, 4))
        self.to = lambda step: device(lax.rem(pos + step * f + 8, 4))
        self.send, self.recv = send, recv

    def copy(self, step, slot, to):
        u = self.unit(step)
        return rcopy(u, u, self.send.at[slot], self.recv.at[slot], self.to(to))

    def start(self):
        self.copy(0, 0, 1).start()
        self.copy(0, 1, -1).start()
        if self.direct:
            self.copy(0, 2, 2).start()

    def forward(self):
        self.copy(-1, 0, 1).wait_recv()
        if not self.direct:
            self.copy(-1, 2, 1).start()

    def near(self):
        self.copy(1, 1, -1).wait_recv()

    def far(self):
        self.copy(2, 2, 1).wait_recv()

    def drain(self):
        self.copy(0, 0, 1).wait_send()
        self.copy(0, 1, -1).wait_send()
        if self.direct:
            self.copy(0, 2, 2).wait_send()
        else:
            self.copy(-1, 2, 1).wait_send()


class Scatter:
    def __init__(self, chunk, pos, f, device, send, recv, bufs):
        self.chunk = lambda step: chunk(lax.rem(pos + step * f + 8, 4))
        self.to = lambda step: device(lax.rem(pos + step * f + 8, 4))
        self.send, self.recv, self.bufs = send, recv, bufs

    def copy(self, src, slot, to):
        return rcopy(src, self.bufs.at[slot], self.send.at[slot], self.recv.at[slot], self.to(to))

    def start(self):
        self.copy(self.chunk(2), 0, 1).start()
        self.copy(self.chunk(-1), 1, -1).start()

    def middle(self):
        self.copy(self.bufs.at[0], 0, 1).wait_recv()
        self.bufs[3] = (self.bufs[0].astype(F32) + self.chunk(1)[...].astype(F32)).astype(BF16)
        self.copy(self.bufs.at[3], 2, 1).start()

    def total(self):
        self.copy(self.bufs.at[1], 1, -1).wait_recv()
        self.copy(self.bufs.at[2], 2, 1).wait_recv()
        return self.chunk(0)[...].astype(F32) + self.bufs[1].astype(F32) + self.bufs[2].astype(F32)

    def drain(self):
        self.copy(self.chunk(2), 0, 1).wait_send()
        self.copy(self.chunk(-1), 1, -1).wait_send()
        self.copy(self.bufs.at[3], 2, 1).wait_send()


def kernel(
    q_hbm, k_hbm, v_hbm, tok_ref, pat_ref, w_hbm, og_hbm,
    lo, qg, kg, vg, fin,
    kin, qrot, kv, og, ogs, wb, attn, attns, probs, mask, tabs,
    ret, got, own,
    wg, b1a, b1b, r1a, r1b, b2, zs, zr,
    in_sem, halo_s, halo_r, ret_s, ret_r, sib_s, sib_r, wz_s, wz_r,
    ag_s, ag_r, wsib_s, wsib_r, rs_s, rs_r, z_s, z_r, fin_s, fin_r,
):
    dp = lax.axis_index("dp")
    ctx = lax.axis_index("ctx")
    x, zh, y = dp // 8, lax.rem(dp // 4, 2), lax.rem(dp, 4)
    zl, core = ctx // 2, lax.rem(ctx, 2)
    z = zh * 4 + zl
    line = z * 2 + core
    f = 1 - 2 * core

    def device(x_, z_, y_, core_):
        return (x_ * 8 + (z_ // 4) * 4 + y_, lax.rem(z_, 4) * 2 + core_)

    def on_line(at):
        return device(x, at // 2, y, lax.rem(at, 2))

    left, right = on_line(lax.rem(line + 15, 16)), on_line(lax.rem(line + 1, 16))
    sibling = (dp, ctx + f)
    on_x = lambda at: device(at, z, y, core)
    on_y = lambda at: device(x, z, at, core)

    def head_cols(h):
        return pl.ds(h * HD, HD)

    ins = []

    def load(src, dst, sem):
        c = pltpu.make_async_copy(src, dst, in_sem.at[sem])
        c.start()
        return c

    my_half = pl.ds(pl.multiple_of(core * HALF, HALF), HALF)
    in_w = load(w_hbm.at[:, my_half], wb.at[x, zh, y, core], 0)
    in_k = [load(k_hbm.at[:, head_cols(h)], kin.at[h], 1 + h) for h in range(H)]
    in_v = [load(v_hbm.at[:, head_cols(h)], kv.at[h, 1, 1], 9 + h) for h in range(H)]
    in_og = load(og_hbm, og, 17)
    in_q = [load(q_hbm.at[:, head_cols(h)], qrot.at[h], 18 + h) for h in range(H)]

    barrier = pltpu.get_barrier_semaphore()
    for step in range(1, 16):
        pl.semaphore_signal(barrier, inc=1, device_id=on_line(lax.rem(line + step, 16)), device_id_type=MESH)
    for step in range(1, 4):
        pl.semaphore_signal(barrier, inc=1, device_id=on_x(lax.rem(x + step, 4)), device_id_type=MESH)
        pl.semaphore_signal(barrier, inc=1, device_id=on_y(lax.rem(y + step, 4)), device_id_type=MESH)

    lane8 = lax.broadcasted_iota(jnp.int32, (8, HD), 1)
    value = lax.broadcasted_iota(jnp.int32, (8, HD), 0).astype(F32)
    freq = jnp.exp(lax.rem(lane8, 8).astype(F32) * (-math.log(100.0) / 8.0))
    cos_of, sin_of = jnp.cos(value * freq), jnp.sin(value * freq)
    tok = jnp.transpose(jnp.broadcast_to(tok_ref[...].astype(F32), (HD, T))).astype(jnp.int32)
    lane = lax.broadcasted_iota(jnp.int32, (T, HD), 1)
    axis = lax.rem(lane, 32) // 8
    shift = jnp.where(axis < 3, axis * 3, 8)
    coord = lax.shift_right_logical(tok, shift) & jnp.where(axis == 2, 3, 7)

    def look_up(table):
        rows = [table[i : i + 1, :] for i in range(8)]
        for bit in range(3):
            on = (coord & (1 << bit)) != 0
            rows = [jnp.where(on, rows[2 * i + 1], rows[2 * i]) for i in range(len(rows) // 2)]
        return rows[0]

    sine = look_up(sin_of)
    tabs[0] = jnp.where(lane < 64, look_up(cos_of), 1.0)
    tabs[1] = jnp.where(lane < 32, -sine, 0.0)
    tabs[2] = jnp.where((lane >= 32) & (lane < 64), sine, 0.0)

    def rotate(v, sign):
        side = pltpu.roll(v, 96, 1) * tabs[1] + pltpu.roll(v, 32, 1) * tabs[2]
        return v * tabs[0] + side if sign > 0 else v * tabs[0] - side

    for i in range(2):
        b = ctx * 2 + i
        for r in range(6):
            kb = ctx * 2 - 2 + r
            hit = (pat_ref[0, b] == kb) | (pat_ref[1, b] == kb) | (pat_ref[2, b] == kb) | (pat_ref[3, b] == kb)
            fill = jnp.where(hit & (kb >= 0), 0.0, NEG)
            mask[pl.ds(i * BLK, BLK), pl.ds(r * BLK, BLK)] = jnp.full((BLK, BLK), fill, F32)

    in_w.wait()
    pl.semaphore_wait(barrier, 21)

    wz = rcopy(wb.at[x, zh, y, core], wb.at[x, zh, y, core], wz_s, wz_r, device(x, 7 - z, y, core))
    wz.start()
    gathers = []
    for s in range(2):
        half = zh if s == 0 else 1 - zh
        top, bottom = pl.ds(0, 16), pl.ds(16, 16)
        first = (
            Gather(lambda p, half=half, top=top: wb.at[x, half, p, core, top], y, f, on_y, ag_s.at[s, 0], ag_r.at[s, 0], True),
            Gather(lambda p, half=half, bottom=bottom: wb.at[p, half, y, core, bottom], x, f, on_x, ag_s.at[s, 1], ag_r.at[s, 1], True),
        )
        second = (
            Gather(lambda p, half=half, top=top: wb.at[p, half, :, core, top], x, f, on_x, ag_s.at[s, 2], ag_r.at[s, 2]),
            Gather(lambda p, half=half, bottom=bottom: wb.at[:, half, p, core, bottom], y, f, on_y, ag_s.at[s, 3], ag_r.at[s, 3]),
        )
        gathers.append((first, second))

    def share(s, step, who=None):
        half = zh if s == 0 else 1 - zh
        at = core if who is None else who
        px, py = lax.rem(x + step * f + 8, 4), lax.rem(y + step * f + 8, 4)
        a = wb.at[px, half, :, at, pl.ds(0, 16)]
        c = wb.at[:, half, py, at, pl.ds(16, 16)]
        k = step % 4
        return (
            rcopy(a, a, wsib_s.at[s, 0, k], wsib_r.at[s, 0, k], sibling),
            rcopy(c, c, wsib_s.at[s, 1, k], wsib_r.at[s, 1, k], sibling),
        )

    def send_share(s, step):
        for c in share(s, step):
            c.start()

    for g in gathers[0][0]:
        g.start()

    def halo(h):
        return (
            rcopy(kv.at[h, 1], kv.at[h, 2], halo_s.at[0, h], halo_r.at[0, h], left),
            rcopy(kv.at[h, 1], kv.at[h, 0], halo_s.at[1, h], halo_r.at[1, h], right),
        )

    for h in range(H):
        in_k[h].wait()
        kv[h, 1, 0] = rotate(kin[h].astype(F32), 1).astype(BF16)
        in_v[h].wait()
        if h:
            for c in halo(h - 1):
                c.start()
    in_og.wait()
    for c in halo(H - 1):
        c.start()
    other_half = pl.ds(pl.multiple_of((1 - core) * HALF, HALF), HALF)
    ogc = rcopy(og.at[:, other_half], ogs, sib_s.at[8], sib_r.at[8], sibling)
    ogc.start()

    def attn_copy(h):
        return rcopy(attn.at[h], attns.at[h], sib_s.at[h], sib_r.at[h], sibling)

    for h in range(H):
        in_q[h].wait()
        qrot[h] = rotate(qrot[h].astype(F32), 1).astype(BF16)

    wz.wait_recv()
    for g in gathers[1][0]:
        g.start()

    def second_ring(s):
        for g in gathers[s][0]:
            g.forward()
            g.near()
            g.far()
        for g in gathers[s][1]:
            g.start()
        send_share(s, 0)

    second_ring(0)

    def keys(h):
        return kv[h, :, 0].reshape(NK, HD)

    def values(h):
        return kv[h, :, 1].reshape(NK, HD)

    def forward(i, carry):
        heads = [2 * i, 2 * i + 1]
        for h in heads:
            for c in halo(h):
                c.wait_recv()
        done = []
        for h in heads:
            scores = dot(qrot[h], keys(h), NT) * SCALE + mask[...]
            e = jnp.exp(scores - jnp.max(scores, axis=1, keepdims=True))
            p = (e * (1.0 / jnp.sum(e, axis=1, keepdims=True))).astype(BF16)
            done.append((p, dot(p, values(h)).astype(BF16)))
        for h, (p, a) in zip(heads, done):
            probs[h] = p
            attn[h] = a

        def relay(s):
            for g in gathers[s][1]:
                g.forward()
            send_share(s, -1)

        def near(s):
            for g in gathers[s][1]:
                g.near()
            send_share(s, 1)

        @pl.when(i == 0)
        def _():
            second_ring(1)

        @pl.when(i == 1)
        def _():
            relay(0)

        @pl.when(i == 2)
        def _():
            near(0)
            relay(1)

        @pl.when(i == 3)
        def _():
            near(1)

        for h in heads:
            attn_copy(h).start()
        return carry

    lax.fori_loop(0, H // 2, forward, 0)

    def far(s):
        for g in gathers[s][1]:
            g.far()
        send_share(s, 2)

    ogc.wait_recv()

    def weight_term(h, carry):
        attn_copy(h).wait_recv()
        term = dot(attn[h], og[:, my_half], TN) + dot(attns[h], ogs[...], TN)
        wg[h // 2, lax.rem(h, 2)] = (term * (1.0 / 32.0)).astype(BF16).reshape(4, ROWS, HALF)
        return carry

    lax.fori_loop(0, 3, weight_term, 0)
    far(0)
    lax.fori_loop(3, H, weight_term, 0)
    far(1)

    scatters = []
    for s in range(2):
        scatters.append((
            Scatter(lambda p, s=s: wg.at[p, s, :, pl.ds(0, 16)], x, f, on_x, rs_s.at[s, 0], rs_r.at[s, 0], b1a.at[s]),
            Scatter(lambda p, s=s: wg.at[:, s, p, pl.ds(16, 16)], y, f, on_y, rs_s.at[s, 1], rs_r.at[s, 1], b1b.at[s]),
            Scatter(lambda p, s=s: r1a.at[s, p], y, f, on_y, rs_s.at[s, 2], rs_r.at[s, 2], b2.at[s, 0]),
            Scatter(lambda p, s=s: r1b.at[s, p], x, f, on_x, rs_s.at[s, 3], rs_r.at[s, 3], b2.at[s, 1]),
        ))
    for s in range(2):
        scatters[s][0].start()
        scatters[s][1].start()

    for s in range(2):
        for k in range(4):
            step = k if k < 3 else -1
            for c in share(s, step, 1 - core):
                c.wait_recv()

    def give_back(h):
        return (
            rcopy(ret.at[0, h], got.at[1, h], ret_s.at[0, h], ret_r.at[1, h], left),
            rcopy(ret.at[1, h], got.at[0, h], ret_s.at[1, h], ret_r.at[0, h], right),
        )

    def take_back(h):
        return (
            rcopy(ret.at[0, h], got.at[1, h], ret_s.at[0, h], ret_r.at[1, h], right),
            rcopy(ret.at[1, h], got.at[0, h], ret_s.at[1, h], ret_r.at[0, h], left),
        )

    def reduce_plane(s):
        r1a[s] = scatters[s][0].total().astype(BF16)
        scatters[s][2].start()
        r1b[s] = scatters[s][1].total().astype(BF16)
        scatters[s][3].start()

    def middle(s, ring):
        for part in range(2):
            scatters[s][2 * ring + part].middle()

    def backward(i, carry):
        w = wb.at[i]
        heads = [2 * i, 2 * i + 1]
        grads = (
            dot(og[:, :HALF], w[:, :, 0].reshape(2 * HD, HALF), NT)
            + dot(og[:, HALF:], w[:, :, 1].reshape(2 * HD, HALF), NT)
        ).astype(BF16)
        done = []
        for n, h in enumerate(heads):
            grad = grads[:, n * HD : (n + 1) * HD]
            delta = jnp.sum(grad.astype(F32) * attn[h].astype(F32), axis=1, keepdims=True)
            p = probs[h]
            dv = dot(p, grad, TN)
            ds = (p.astype(F32) * ((dot(grad, values(h), NT) - delta) * SCALE)).astype(BF16)
            dk = dot(ds, qrot[h], TN)
            done.append((dv, dk, rotate(dot(ds, keys(h)), -1).astype(BF16)))
        for h, (dv, dk, dq) in zip(heads, done):
            ret[0, h, 1] = dv[:T].astype(BF16)
            own[h, 1] = dv[T : 2 * T]
            ret[1, h, 1] = dv[2 * T :].astype(BF16)
            ret[0, h, 0] = dk[:T].astype(BF16)
            own[h, 0] = dk[T : 2 * T]
            ret[1, h, 0] = dk[2 * T :].astype(BF16)
            qg[h] = dq
        for h in heads:
            for c in give_back(h):
                c.start()

        @pl.when(i == 1)
        def _():
            middle(0, 0)

        @pl.when(i == 2)
        def _():
            middle(1, 0)

        return carry

    lax.fori_loop(0, H // 2, backward, 0)
    reduce_plane(0)
    reduce_plane(1)

    rows = jnp.concatenate([attn[h] for h in range(H)], axis=1)

    def project(j, carry):
        cols = pl.ds(pl.multiple_of(lax.rem(j, 4) * 256, 256), 256)
        w = wb[:, :, :, j // 4, :, cols].reshape(H * HD, 256)
        lo[:, pl.ds(pl.multiple_of(j * 256, 256), 256)] = dot(rows, w).astype(BF16)

        return carry

    lax.fori_loop(0, 3, project, 0)
    for s in range(2):
        middle(s, 1)

    def finish(h, carry):
        for c in take_back(h):
            c.wait_recv()
        dk = own[h, 0] + got[0, h, 0].astype(F32) + got[1, h, 0].astype(F32)
        dv = own[h, 1] + got[0, h, 1].astype(F32) + got[1, h, 1].astype(F32)
        kg[h] = rotate(dk, -1).astype(BF16)
        vg[h] = dv.astype(BF16)
        return carry

    lax.fori_loop(0, H, finish, 0)

    for s in range(2):
        for part in range(2):
            done = scatters[s][2 + part].total().astype(BF16)
            for j in range(4):
                zs[s * 4 + j, pl.ds(part * 16, 16)] = done[:, j * 256 : (j + 1) * 256]

    def z_copy(step):
        to = lax.rem(z + step, 8)
        return rcopy(zs.at[to], zr.at[step - 1], z_s.at[step - 1], z_r.at[step - 1], device(x, to, y, core))

    for step in range(1, 8):
        z_copy(step).start()

    lax.fori_loop(3, 8, project, 0)
    for step in range(1, 8):
        z_copy(step).wait_recv()
    total = zs[z].astype(F32)
    for step in range(7):
        total = total + zr[step].astype(F32)
    fin[ctx] = total.astype(BF16)

    def fin_copy(step):
        to = lax.rem(ctx + step, 8)
        return rcopy(fin.at[ctx], fin.at[ctx], fin_s.at[step - 1], fin_r.at[step - 1], (dp, to))

    def fin_from(step):
        who = lax.rem(ctx + 8 - step, 8)
        return rcopy(fin.at[who], fin.at[who], fin_s.at[step - 1], fin_r.at[step - 1], (dp, who))

    for step in range(1, 8):
        fin_copy(step).start()
    for step in range(1, 8):
        fin_from(step).wait_recv()

    wz.wait_send()
    ogc.wait_send()
    for h in range(H):
        attn_copy(h).wait_send()
        for c in (*halo(h), *give_back(h)):
            c.wait_send()
    for s in range(2):
        for g in (*gathers[s][0], *gathers[s][1], *scatters[s]):
            g.drain()
        for k in range(4):
            for c in share(s, k if k < 3 else -1):
                c.wait_send()
    for step in range(1, 8):
        z_copy(step).wait_send()
        fin_copy(step).wait_send()


def write(lo, qg, kg, vg, fin, lo_hbm, qg_hbm, kg_hbm, vg_hbm, wg_hbm, wide, sem):
    copies = []

    def store(src, dst):
        copies.append(pltpu.make_async_copy(src, dst, sem.at[len(copies)]))
        copies[-1].start()

    store(lo, lo_hbm)
    for h in range(H):
        cols = pl.ds(h * HD, HD)
        for src, dst in ((qg, qg_hbm), (kg, kg_hbm), (vg, vg_hbm)):
            store(src.at[h], dst.at[:, cols])
    wide[...] = fin[...].astype(F32)
    for c in range(8):
        store(wide.at[c], wg_hbm.at[:, pl.ds((c % 2) * HALF + (c // 2) * 256, 256)])
    for c in copies:
        c.wait()


def shards(queries, key_states, value_states, token_order, block_pattern, out_weight, out_grad):
    any_ = pl.BlockSpec(memory_space=pl.ANY)
    hbm = lambda array: pltpu.with_memory_space_constraint(array, pltpu.HBM)
    vmem = pl.BlockSpec(memory_space=pltpu.VMEM)
    smem = pl.BlockSpec(memory_space=pltpu.SMEM)
    dma = pltpu.SemaphoreType.DMA
    V = pltpu.VMEM
    token_rows = jax.ShapeDtypeStruct((T, H * HD), BF16)
    out = pl.pallas_call(
        kernel,
        out_shape=(
            V((T, D), BF16),
            V((H, T, HD), BF16),
            V((H, T, HD), BF16),
            V((H, T, HD), BF16),
            V((8, ROWS, 256), BF16),
        ),
        in_specs=[any_, any_, any_, vmem, smem, any_, any_],
        out_specs=(vmem,) * 5,
        scratch_shapes=[
            V((H, T, HD), BF16),
            V((H, T, HD), BF16),
            V((H, 3, 2, T, HD), BF16),
            V((T, D), BF16),
            V((T, HALF), BF16),
            V((4, 2, 4, 2, ROWS, HALF), BF16),
            V((H, T, HD), BF16),
            V((H, T, HD), BF16),
            V((H, T, NK), BF16),
            V((T, NK), F32),
            V((3, T, HD), F32),
            V((2, H, 2, T, HD), BF16),
            V((2, H, 2, T, HD), BF16),
            V((H, 2, T, HD), F32),
            V((4, 2, 4, ROWS, HALF), BF16),
            V((2, 4, 4, 16, HALF), BF16),
            V((2, 4, 4, 16, HALF), BF16),
            V((2, 4, 16, HALF), BF16),
            V((2, 4, 16, HALF), BF16),
            V((2, 2, 4, 16, HALF), BF16),
            V((8, ROWS, 256), BF16),
            V((7, ROWS, 256), BF16),
            dma((26,)),
            dma((2, H)), dma((2, H)), dma((2, H)), dma((2, H)),
            dma((9,)), dma((9,)), dma(()), dma(()),
            dma((2, 4, 3)), dma((2, 4, 3)), dma((2, 2, 4)), dma((2, 2, 4)),
            dma((2, 4, 3)), dma((2, 4, 3)), dma((7,)), dma((7,)), dma((7,)), dma((7,)),
        ],
        compiler_params=pltpu.CompilerParams(
            collective_id=0, has_side_effects=True, vmem_limit_bytes=LIMIT
        ),
    )(
        hbm(queries[0]),
        hbm(key_states[0]),
        hbm(value_states[0]),
        token_order,
        jnp.transpose(block_pattern[0]),
        hbm(out_weight),
        hbm(out_grad[0]),
    )
    lo, qg, kg, vg, wg = pl.pallas_call(
        write,
        out_shape=(
            jax.ShapeDtypeStruct((T, D), BF16),
            token_rows,
            token_rows,
            token_rows,
            jax.ShapeDtypeStruct((ROWS, D), F32),
        ),
        in_specs=[vmem] * 5,
        out_specs=(any_,) * 5,
        scratch_shapes=[V((8, ROWS, 256), F32), dma((33,))],
        compiler_params=pltpu.CompilerParams(vmem_limit_bytes=LIMIT),
    )(*(pltpu.with_memory_space_constraint(o, pltpu.VMEM) for o in out))
    return lo[None], qg[None], kg[None], vg[None], wg


def solution(mesh):
    rows = P("dp", "ctx", None)
    in_specs = (rows, rows, rows, P("dp", "ctx"), P("dp", None, None), P("dp", None), rows)
    out_specs = (rows, rows, rows, rows, P("dp", None))
    return jax.shard_map(shards, mesh=mesh, in_specs=in_specs, out_specs=out_specs, check_vma=False)
```
